256 devices in a mesh: section: 4 (over z_hi), dp: 16 (over x, z_lo, core), feat: 4 (over y).
Axes of the slice: x: 4, y: 4, z: 8 (z_hi: 4, z_lo: 2; z = z_hi * 2 + z_lo), core: 2. Of those that a mesh axis runs over, the one named last changes fastest.
Arguments:
- tokens: bfloat16 [4096, 16384], P('dp', 'feat'), may hold values from -6 to 6
- basis: bfloat16 [2048, 16384], P('section', 'feat'), may hold values from -0.046875 to 0.046875
Outputs:
- basis_step: bfloat16 [2048, 16384], P('section', 'feat')
- projections: float32 [4096, 2048], P('dp', 'section')
The draws below stay inside these ranges and needn't reach their ends.
All inputs are finite; a program needn't handle non-finite values.
Results may differ from the reference program's by a relative error of at most 0.034.
Values may be sent and summed in bfloat16 or wider, within the bound.
A program may use at most 64 MiB of HBM per device.

```python
import math
import jax
import jax.numpy as jnp
from jax import lax

D = 16384
BLOCK = 512
ROWS_DEV = 256
ROWS = 4096
COMPS = 2048
N_SECTION = 4
N_DP = 16


def levels(stream_key, dims, split, low, largest):
    def one(position, blocks):
        steps = jax.random.uniform(jax.random.fold_in(jax.random.fold_in(stream_key, 6), position), (blocks,), jnp.float32, low / len(split), largest / len(split))
        return jnp.repeat(jnp.exp(steps), dims[position] // blocks).reshape((-1,) + (1,) * (len(dims) - position - 1))

    level = one(*split[0])
    for cut in split[1:]:
        level = level * one(*cut)
    return level


def scatter_about(key, dims, spread, reach, split=(), held_as=jnp.bfloat16):
    drawn = jax.random.normal(key, dims, jnp.float32) * spread
    if len(split) > 0:
        drawn = levels(key, dims, split, -0.22, 0.18) * drawn
    return jnp.clip(drawn, min=-reach, max=reach).astype(held_as)


def setup_inputs(seed: int = 0) -> dict:
    keys = jax.random.split(jax.random.key(seed), 3)
    tokens = scatter_about(keys[0], (ROWS, D), 1.0, 6.0, ((0, 16), (1, 4)))
    basis = scatter_about(keys[1], (COMPS, D), D ** -0.5, 0.046875, ((0, 4), (1, 4)))
    return {"tokens": tokens, "basis": basis}


def group_sum(left, right):
    total = jnp.zeros((left.shape[1], right.shape[1]), jnp.float32)
    for group in range(N_DP):
        left_rows = left[group * ROWS_DEV:(group + 1) * ROWS_DEV]
        right_rows = right[group * ROWS_DEV:(group + 1) * ROWS_DEV]
        partial_value = lax.dot_general(left_rows, right_rows, (((0,), (0,)), ((), ())), preferred_element_type=jnp.float32)
        rounded = lax.optimization_barrier(partial_value.astype(jnp.bfloat16))
        total = total + rounded.astype(jnp.float32)
    return total

def reference(tokens, basis):
    scaling = math.sqrt(D) / (ROWS_DEV * N_DP)
    residual = tokens
    steps_out = []
    scores_out = []
    for block_id in range(N_SECTION):
        weights = basis[block_id * BLOCK:(block_id + 1) * BLOCK]
        scores = lax.dot_general(residual, weights, (((1,), (1,)), ((), ())), preferred_element_type=jnp.float32)
        rounded = scores.astype(jnp.bfloat16)
        hebbian = group_sum(rounded, residual)
        covariance = group_sum(rounded, rounded)
        triangle = jnp.tril(covariance).astype(jnp.bfloat16)
        damping = jnp.dot(triangle, weights, preferred_element_type=jnp.float32)
        steps_out.append(((hebbian - damping) * scaling).astype(jnp.bfloat16))
        scores_out.append(scores)
        residual = (residual.astype(jnp.float32) - jnp.dot(rounded, weights, preferred_element_type=jnp.float32)).astype(jnp.bfloat16)
    return (jnp.concatenate(steps_out, axis=0), jnp.concatenate(scores_out, axis=1))
```

```python
import math

import jax
import jax.numpy as jnp
from jax import lax
from jax.sharding import PartitionSpec as P

D = 16384
BF16 = jnp.bfloat16
F32 = jnp.float32


def dot(a, b, ca, cb):
    return lax.dot_general(a, b, (((ca,), (cb,)), ((), ())), preferred_element_type=F32)


def shards(tokens, basis):
    s = lax.axis_index("section")
    d = lax.axis_index("dp")
    n_sec = lax.axis_size("section")
    n_dp = lax.axis_size("dp")
    rows, width = tokens.shape
    block = basis.shape[0]
    piece = block // n_dp
    scaling = math.sqrt(D) / (rows * n_dp)

    mine = lax.dynamic_slice_in_dim(basis, d * piece, piece, 0)
    slices = lax.all_gather(mine, "section").reshape(n_sec * piece, width)
    cross = dot(slices, basis, 1, 1).astype(BF16)
    cross = lax.psum(cross, "feat")
    cross = lax.all_gather(cross, ("section", "dp"))
    cross = cross.reshape(n_sec, n_dp, n_sec, piece, block)
    cross = cross.transpose(0, 2, 1, 3, 4).reshape(n_sec, n_sec, block, block)

    scores = dot(tokens, basis, 1, 1).astype(BF16)
    scores = lax.psum_scatter(scores, "feat", scatter_dimension=0, tiled=True)
    scores = lax.all_gather(scores, "section")
    rounded = []
    for b in range(n_sec):
        y = scores[b].astype(F32)
        for j in range(b):
            y = y - dot(rounded[j], cross[b, j], 1, 0)
        rounded.append(y.astype(BF16))
    q = jnp.stack(rounded)
    q = lax.all_gather(q, "feat", axis=1, tiled=True)
    q_mine = lax.dynamic_index_in_dim(q, s, 0, keepdims=False)
    projections = q_mine.astype(F32)

    gram = jnp.einsum("jrc,rk->jck", q, q_mine, preferred_element_type=F32)
    gram = gram.astype(BF16).reshape(n_sec, n_dp, piece, block).transpose(1, 0, 2, 3)
    gram = lax.psum_scatter(gram, "dp", scatter_dimension=0, tiled=True)[0]
    col = d * piece + lax.broadcasted_iota(jnp.int32, (n_sec, piece, block), 1)
    row = lax.broadcasted_iota(jnp.int32, (n_sec, piece, block), 2)
    j = lax.broadcasted_iota(jnp.int32, (n_sec, piece, block), 0)
    keep = (j < s) | ((j == s) & (col <= row))
    gram = jnp.where(keep, gram, jnp.zeros_like(gram)).reshape(n_sec * piece, block)
    part = dot(q_mine, tokens, 0, 0) - dot(gram, slices, 0, 0)
    total = lax.psum(part.astype(BF16), "dp")
    basis_step = (total.astype(F32) * scaling).astype(BF16)
    return basis_step, projections


def solution(mesh):
    in_specs = (P("dp", "feat"), P("section", "feat"))
    out_specs = (P("section", "feat"), P("dp", "section"))
    return jax.shard_map(shards, mesh=mesh, in_specs=in_specs, out_specs=out_specs, check_vma=False)
```

```python
import functools
import math

import jax
import jax.numpy as jnp
from jax import lax
from jax.experimental import pallas as pl
from jax.experimental.pallas import tpu as pltpu
from jax.sharding import PartitionSpec as P

D = 16384
BF16 = jnp.bfloat16
F32 = jnp.float32
MESH = pl.DeviceIdType.MESH
ROWS = 256
WIDTH = 4096
BLOCK = 512
H = 256
SCALE = math.sqrt(D) / 4096


def dot(a, b, ca, cb):
    return lax.dot_general(a, b, (((ca,), (cb,)), ((), ())), preferred_element_type=F32)


def at(start, size):
    return pl.ds(pl.multiple_of(start, size), size)


def kernel(
    tokens, basis, out, proj,
    tok, tok_other, w, wz, tpart, trecv, tall, upart, urecv, u, q, gpart, grecv, gfull,
    ahalf, afull, az, s1, p2, xa, xb, xc, e2, zb,
    ssem, lsem, r_tok, r_w, r_t, r_ta, r_u, r_us, r_ux, r_uc, r_q, r_qc, r_g, r_ga,
    r_az, r_xa, r_xb, r_xc, r_zb, r_o1x, r_o1z, r_o2z, r_o2x, r_oc,
):
    s = lax.axis_index("section")
    d = lax.axis_index("dp")
    f = lax.axis_index("feat")
    x, z, c = d // 4, (d // 2) % 2, d % 2
    xz = d // 2
    zo, co = 1 - z, 1 - c

    def dev(s=s, x=x, z=z, c=c, f=f):
        return (s, x * 4 + z * 2 + c, f)

    pending = []

    def when(cond, do):
        if cond is None:
            do()
        else:
            pl.when(cond)(do)

    def send(src, dst, target, sem, cond=None):
        copy = pltpu.make_async_remote_copy(
            src_ref=src, dst_ref=dst, send_sem=ssem.at[len(pending)], recv_sem=sem,
            device_id=target, device_id_type=MESH,
        )
        when(cond, copy.start)
        pending.append((copy, cond))

    def arrived(dst, sem, cond=None):
        when(cond, pltpu.make_async_copy(dst, dst, sem).wait)

    feats = at((2 * c + z) * 1024, 1024)
    load_tok = pltpu.make_async_copy(tokens, tok, lsem.at[0])
    load_w = pltpu.make_async_copy(basis, w, lsem.at[1])
    load_z = pltpu.make_async_copy(basis.at[at(x * 128, 128), feats], wz.at[at(s * 128, 128)], lsem.at[2])
    load_tok.start()
    load_w.start()
    load_z.start()

    group = f * 4 + z * 2 + c
    sections = [dev(s=(s + k) % 4) for k in range(1, 4)]
    sixteen = []
    for k in range(1, 16):
        g = (group + k) % 16
        sixteen.append((g, dev(f=g // 4, z=(g // 2) % 2, c=g % 2)))
    planes = []
    for k in range(1, 8):
        p = (xz // 2 + k // 2) % 4 * 2 + (z + k) % 2
        planes.append((p, dev(x=p // 2, z=p % 2)))
    barrier = pltpu.get_barrier_semaphore()
    friends = sections + [t for _, t in sixteen] + [t for k, (_, t) in enumerate(planes, 1) if k // 2 > 0]
    for target in friends:
        pl.semaphore_signal(barrier, inc=1, device_id=target, device_id_type=MESH)
    for j in range(3):
        def clear(j=j):
            upart[j] = jnp.zeros((128, 512), BF16)
        pl.when(j >= s)(clear)
    for j in range(1, 4):
        def clear(j=j):
            wz[j * 128:(j + 1) * 128] = jnp.zeros((128, 1024), BF16)
        pl.when(j > s)(clear)
    pl.semaphore_wait(barrier, len(friends))

    for k in (3, 2, 1):
        send(basis.at[at(x * 128, 128), feats], wz.at[at(s * 128, 128)], dev(s=(s + k) % 4), r_w.at[s], s + k < 4)
    load_tok.wait()
    send(tok.at[:, at(co * 2048, 2048)], tok_other, dev(c=co), r_tok)
    load_w.wait()

    def score(t, carry):
        cols = at(t * 128, 128)
        tpart[:, cols] = dot(tok[...], w[cols, :], 1, 1).astype(BF16)
        return carry
    lax.fori_loop(0, 4, score, 0)
    for k in range(1, 4):
        g = (f + k) % 4
        send(tpart.at[:, at(g * 128, 128)], trecv.at[f], dev(f=g), r_t.at[f])
    total = tpart[:, at(f * 128, 128)].astype(F32)
    for k in range(1, 4):
        g = (f + k) % 4
        arrived(trecv.at[g], r_t.at[g])
        total = total + trecv[g].astype(F32)
    tall[s] = total.astype(BF16)
    for k in (3, 2, 1):
        send(tall.at[s], tall.at[s], dev(s=(s + k) % 4), r_ta.at[s], s + k < 4)

    load_z.wait()
    for j in range(3):
        def cross(j=j):
            arrived(wz.at[pl.ds(j * 128, 128)], r_w.at[j])
            upart[j] = dot(wz[j * 128:(j + 1) * 128], w[:, feats], 1, 1).astype(BF16)
        pl.when(j < s)(cross)
    some = s > 0
    for g, target in sixteen:
        send(upart.at[:, at(g % 4 * 32, 32), at(g // 4 * 128, 128)], urecv.at[group], target, r_u.at[group], some)

    def step(b):
        def do():
            arrived(tall.at[b], r_ta.at[b], b < s)
            y = tall[b].astype(F32)
            for j in range(b):
                y = y - dot(q[c, j], u[b * (b - 1) // 2 + j].reshape(BLOCK, 128), 1, 0)
            q[c, b, :, at(f * 128, 128)] = y.astype(BF16)
        need = b <= s
        pl.when(need)(do)
        for k in range(1, 4):
            mine = q.at[c, b, :, at(f * 128, 128)]
            send(mine, mine, dev(f=(f + k) % 4), r_q.at[b * 4 + f], need)
        for k in range(1, 4):
            g = (f + k) % 4
            arrived(q.at[c, b, :, at(g * 128, 128)], r_q.at[b * 4 + g], need)
        send(q.at[c, b], q.at[c, b], dev(c=co), r_qc.at[b], need)

    step(0)

    def reduce_cross():
        total = upart[:, at(group % 4 * 32, 32), at(f * 128, 128)].astype(F32)
        for g, _ in sixteen:
            arrived(urecv.at[g], r_u.at[g])
            total = total + urecv[g].astype(F32)
        total = total.astype(BF16)
        for b in range(1, 4):
            def put(b=b):
                for j in range(b):
                    u[b * (b - 1) // 2 + j, xz, c] = total[j]
            pl.when(s == b)(put)
    pl.when(some)(reduce_cross)
    one, two, three = u.at[pl.ds(0, 1), xz, c], u.at[pl.ds(1, 2), xz, c], u.at[pl.ds(0, 6), xz, c]
    send(one, one, dev(s=3), r_us.at[0], s == 1)
    send(one, one, dev(s=2), r_us.at[0], s == 1)
    send(two, two, dev(s=3), r_us.at[1], s == 2)
    arrived(one, r_us.at[0], s >= 2)
    arrived(two, r_us.at[1], s == 3)
    for b in range(1, 4):
        n = b * (b + 1) // 2
        for p, target in planes:
            mine = u.at[pl.ds(0, n), xz, c]
            send(mine, mine, target, r_ux.at[xz], s == b)
        for p, _ in planes:
            arrived(u.at[pl.ds(0, n), p, c], r_ux.at[p], s == b)
        both = u.at[pl.ds(0, n), :, c]
        send(both, both, dev(c=co), r_uc, s == b)
        arrived(u.at[pl.ds(0, n), :, co], r_uc, s == b)

    for b in range(1, 4):
        step(b)
    for b in range(4):
        arrived(q.at[co, b], r_qc.at[b], b <= s)
    proj[...] = q[c, s].astype(F32)

    for j in range(4):
        def gram(j=j):
            cols = at(f * 128, 128)
            g = dot(q[0, j], q[0, s, :, cols], 0, 0) + dot(q[1, j], q[1, s, :, cols], 0, 0)
            gpart[j] = g.astype(BF16).reshape(8, 2, 32, 128)
        pl.when(j <= s)(gram)

        def none(j=j):
            gpart[j] = jnp.zeros((8, 2, 32, 128), BF16)
        pl.when(j > s)(none)
    for p, target in planes:
        send(gpart.at[:, p, c], grecv.at[xz], target, r_g.at[xz])

    arrived(tok_other, r_tok)
    turned = [q[k, s].T for k in range(2)]
    mine_q = jnp.where(c == 0, turned[0], turned[1])
    other_q = jnp.where(c == 0, turned[1], turned[0])

    def hebb(t, half):
        here = dot(mine_q, tok[:, at(c * 2048 + half * 1024 + t * 256, 256)], 1, 0)
        there = dot(other_q, tok_other[:, at(half * 1024 + t * 256, 256)], 1, 0)
        return here + there

    def first(t, carry):
        ahalf[:, at(t * 256, 256)] = hebb(t, zo).astype(BF16)
        return carry
    lax.fori_loop(0, 4, first, 0)
    send(ahalf.at[pl.ds(0, H)], az, dev(z=zo), r_az)
    for k in range(1, 4):
        g = (x + k) % 4
        send(ahalf.at[pl.ds(H, BLOCK - H), at(g * 256, 256)], xb.at[x], dev(x=g), r_xb.at[x])

    def second(t, carry):
        afull[:, at(t * 256, 256)] = hebb(t, z)
        return carry
    lax.fori_loop(0, 4, second, 0)

    total = gpart[:, xz, c].astype(F32)
    for p, _ in planes:
        arrived(grecv.at[p], r_g.at[p])
        total = total + grecv[p].astype(F32)
    shape = (4, 32, 128)
    block = lax.broadcasted_iota(jnp.int32, shape, 0)
    col = d * 32 + lax.broadcasted_iota(jnp.int32, shape, 1)
    row = f * 128 + lax.broadcasted_iota(jnp.int32, shape, 2)
    keep = (block < s) | ((block == s) & (col <= row))
    gfull[:, at(group % 4 * 32, 32), at(f * 128, 128)] = jnp.where(keep, total, 0.0).astype(BF16)
    mine = gfull.at[:, at(group % 4 * 32, 32), at(f * 128, 128)]
    for g, target in sixteen:
        send(mine, mine, target, r_ga.at[group])
    for g, _ in sixteen:
        arrived(gfull.at[:, at(g % 4 * 32, 32), at(g // 4 * 128, 128)], r_ga.at[g])
    lower = gfull[...].reshape(512, BLOCK).T

    def damp(t, carry):
        cols = at(t * 256, 256)
        afull[:, cols] = afull[:, cols] - dot(lower, wz[:, cols], 1, 0)
        return carry
    lax.fori_loop(0, 4, damp, 0)

    mycols = at(x * 256, 256)
    p2[...] = afull[H:].astype(BF16)
    for k in range(1, 4):
        g = (x + k) % 4
        send(p2.at[:, at(g * 256, 256)], xc.at[x], dev(x=g), r_xc.at[x])
    arrived(az, r_az)
    afull[:H] = afull[:H] + az[...].astype(F32)
    s1[...] = afull[:H].astype(BF16)
    for k in range(1, 4):
        g = (x + k) % 4
        send(s1.at[:, at(g * 256, 256)], xa.at[x], dev(x=g), r_xa.at[x])
    total = ahalf[H:, mycols].astype(F32)
    for k in range(1, 4):
        g = (x + k) % 4
        arrived(xb.at[g], r_xb.at[g])
        total = total + xb[g].astype(F32)
    e2[...] = total.astype(BF16)
    send(e2, zb, dev(z=zo), r_zb)
    total = afull[H:, mycols]
    for k in range(1, 4):
        g = (x + k) % 4
        arrived(xc.at[g], r_xc.at[g])
        total = total + xc[g].astype(F32)
    arrived(zb, r_zb)
    total = total + zb[...].astype(F32)

    def cols_of(x, z, n=256):
        return at(c * 2048 + z * 1024 + x * 256, n)

    top, low = pl.ds(0, H), pl.ds(H, BLOCK - H)
    out[H:, cols_of(x, z)] = (total * SCALE).astype(BF16)
    mine = out.at[low, cols_of(x, z)]
    send(mine, mine, dev(z=zo), r_o2z)
    for k in range(1, 4):
        send(mine, mine, dev(x=(x + k) % 4), r_o2x.at[x])
    total = afull[:H, mycols]
    for k in range(1, 4):
        g = (x + k) % 4
        arrived(xa.at[g], r_xa.at[g])
        total = total + xa[g].astype(F32)
    out[:H, cols_of(x, z)] = (total * SCALE).astype(BF16)
    mine = out.at[top, cols_of(x, z)]
    for k in range(1, 4):
        send(mine, mine, dev(x=(x + k) % 4), r_o1x.at[x])
    other = out.at[low, cols_of(x, zo)]
    arrived(other, r_o2z)
    for k in range(1, 4):
        send(other, other, dev(x=(x + k) % 4), r_o2x.at[4 + x])
    for k in range(1, 4):
        g = (x + k) % 4
        arrived(out.at[top, cols_of(g, z)], r_o1x.at[g])
    mine = out.at[top, at(c * 2048 + z * 1024, 1024)]
    send(mine, mine, dev(z=zo), r_o1z)
    send(mine, mine, dev(c=co), r_oc.at[0])
    for k in range(1, 4):
        g = (x + k) % 4
        arrived(out.at[low, cols_of(g, z)], r_o2x.at[g])
    mine = out.at[low, at(c * 2048 + z * 1024, 1024)]
    send(mine, mine, dev(c=co), r_oc.at[1])
    for k in range(1, 4):
        g = (x + k) % 4
        arrived(out.at[low, cols_of(g, zo)], r_o2x.at[4 + g])
    mine = out.at[low, at(c * 2048 + zo * 1024, 1024)]
    send(mine, mine, dev(c=co), r_oc.at[2])
    mine = out.at[top, at(c * 2048 + zo * 1024, 1024)]
    arrived(mine, r_o1z)
    send(mine, mine, dev(c=co), r_oc.at[3])
    arrived(out.at[top, at(co * 2048 + z * 1024, 1024)], r_oc.at[0])
    arrived(out.at[low, at(co * 2048 + z * 1024, 1024)], r_oc.at[1])
    arrived(out.at[low, at(co * 2048 + zo * 1024, 1024)], r_oc.at[2])
    arrived(out.at[top, at(co * 2048 + zo * 1024, 1024)], r_oc.at[3])
    for copy, cond in pending:
        when(cond, copy.wait_send)


def shards(tokens, basis):
    dma = pltpu.SemaphoreType.DMA
    vm = pltpu.VMEM
    out, proj = pl.pallas_call(
        kernel,
        out_shape=(
            jax.ShapeDtypeStruct((BLOCK, WIDTH), BF16),
            jax.ShapeDtypeStruct((ROWS, BLOCK), F32),
        ),
        in_specs=[pl.BlockSpec(memory_space=pl.ANY)] * 2,
        out_specs=(pl.BlockSpec(memory_space=pltpu.VMEM), pl.BlockSpec(memory_space=pltpu.VMEM)),
        scratch_shapes=[
            vm((ROWS, WIDTH), BF16),
            vm((ROWS, 2048), BF16),
            vm((BLOCK, WIDTH), BF16),
            vm((512, 1024), BF16),
            vm((ROWS, BLOCK), BF16),
            vm((4, ROWS, 128), BF16),
            vm((4, ROWS, 128), BF16),
            vm((3, 128, 512), BF16),
            vm((16, 3, 32, 128), BF16),
            vm((6, 8, 2, 32, 128), BF16),
            vm((2, 4, ROWS, BLOCK), BF16),
            vm((4, 8, 2, 32, 128), BF16),
            vm((8, 4, 32, 128), BF16),
            vm((4, 128, 512), BF16),
            vm((BLOCK, 1024), BF16),
            vm((BLOCK, 1024), F32),
            vm((H, 1024), BF16),
            vm((H, 1024), BF16),
            vm((BLOCK - H, 1024), BF16),
            vm((4, H, 256), BF16),
            vm((4, BLOCK - H, 256), BF16),
            vm((4, BLOCK - H, 256), BF16),
            vm((BLOCK - H, 256), BF16),
            vm((BLOCK - H, 256), BF16),
            dma((160,)),
            dma((3,)),
            dma,
            dma((4,)),
            dma((4,)),
            dma((4,)),
            dma((16,)),
            dma((2,)),
            dma((8,)),
            dma,
            dma((16,)),
            dma((4,)),
            dma((8,)),
            dma((16,)),
            dma,
            dma((4,)),
            dma((4,)),
            dma((4,)),
            dma,
            dma((4,)),
            dma,
            dma,
            dma((8,)),
            dma((4,)),
        ],
        compiler_params=pltpu.CompilerParams(
            collective_id=0, has_side_effects=True, vmem_limit_bytes=56 << 20
        ),
        name="sanger",
    )(tokens, basis)
    return out, proj


def solution(mesh):
    in_specs = (P("dp", "feat"), P("section", "feat"))
    out_specs = (P("section", "feat"), P("dp", "section"))
    return jax.shard_map(shards, mesh=mesh, in_specs=in_specs, out_specs=out_specs, check_vma=False)
```

```python
import functools
import math

import jax
import jax.numpy as jnp
from jax import lax
from jax.experimental import pallas as pl
from jax.experimental.pallas import tpu as pltpu
from jax.sharding import PartitionSpec as P

D = 16384
BF16 = jnp.bfloat16
F32 = jnp.float32
MESH = pl.DeviceIdType.MESH
ROWS = 256
WIDTH = 4096
BLOCK = 512
H = 128
TOP = 224
SCALE = math.sqrt(D) / 4096


def dot(a, b, ca, cb):
    return lax.dot_general(a, b, (((ca,), (cb,)), ((), ())), preferred_element_type=F32)


def at(start, size):
    return pl.ds(pl.multiple_of(start, size), size)


def kernel(
    tokens, basis, out, proj,
    tok, tok_other, w, wz, tpart, trecv, tall, upart, urecv, u, q, gpart, grecv, gfull,
    ahalf, afull, az, s1, p2, xa, xb, xc, e2, zb,
    ssem, lsem, r_tok, r_w, r_t, r_ta, r_u, r_us, r_ux, r_uc, r_q, r_qc, r_g, r_ga,
    r_az, r_xa, r_xb, r_xc, r_zb, r_ox, r_oz, r_oc, r_w0,
):
    s = lax.axis_index("section")
    d = lax.axis_index("dp")
    f = lax.axis_index("feat")
    x, z, c = d // 4, (d // 2) % 2, d % 2
    xz = d // 2
    zo, co = 1 - z, 1 - c

    def dev(s=s, x=x, z=z, c=c, f=f):
        return (s, x * 4 + z * 2 + c, f)

    pending = []

    def when(cond, do):
        if cond is None:
            do()
        else:
            pl.when(cond)(do)

    def send(src, dst, target, sem, cond=None):
        copy = pltpu.make_async_remote_copy(
            src_ref=src, dst_ref=dst, send_sem=ssem.at[len(pending)], recv_sem=sem,
            device_id=target, device_id_type=MESH,
        )
        when(cond, copy.start)
        pending.append((copy, cond))

    def arrived(dst, sem, cond=None):
        when(cond, pltpu.make_async_copy(dst, dst, sem).wait)

    feats = at((2 * c + z) * 1024, 1024)
    load_tok = pltpu.make_async_copy(tokens, tok, lsem.at[0])
    load_w = pltpu.make_async_copy(basis, w, lsem.at[1])
    load_z = pltpu.make_async_copy(basis.at[at(x * 128, 128), feats], wz.at[at(s * 128, 128)], lsem.at[2])
    load_tok.start()
    load_w.start()
    load_z.start()

    group = f * 4 + z * 2 + c
    sections = [dev(s=(s + k) % 4) for k in range(1, 4)]
    sixteen = []
    for k in range(1, 16):
        g = (group + k) % 16
        sixteen.append((g, dev(f=g // 4, z=(g // 2) % 2, c=g % 2)))
    planes = []
    for k in range(1, 8):
        p = (xz // 2 + k // 2) % 4 * 2 + (z + k) % 2
        planes.append((p, dev(x=p // 2, z=p % 2)))
    barrier = pltpu.get_barrier_semaphore()
    friends = sections + [t for _, t in sixteen] + [t for k, (_, t) in enumerate(planes, 1) if k // 2 > 0]
    for target in friends:
        pl.semaphore_signal(barrier, inc=1, device_id=target, device_id_type=MESH)
    for j in range(3):
        def clear(j=j):
            upart[j] = jnp.zeros((128, 512), BF16)
        pl.when(j >= s)(clear)
    for j in range(1, 4):
        def clear(j=j):
            wz[j * 128:(j + 1) * 128] = jnp.zeros((128, 1024), BF16)
        pl.when(j > s)(clear)
    pl.semaphore_wait(barrier, len(friends))

    for n in range(4):
        for b in (3, 1):
            send(basis.at[at(x * 128 + n * 32, 32), feats], wz.at[pl.ds(n * 32, 32)], dev(s=b), r_w0.at[n], s == 0)
    for k in (2, 1):
        send(basis.at[at(x * 128, 128), feats], wz.at[at(s * 128, 128)], dev(s=(s + k) % 4), r_w.at[s], (s > 0) & (s + k < 4))
    load_tok.wait()
    send(tok.at[:, at(co * 2048, 2048)], tok_other, dev(c=co), r_tok)
    load_w.wait()

    def score(t, carry):
        cols = at(t * 128, 128)
        tpart[:, cols] = dot(tok[...], w[cols, :], 1, 1).astype(BF16)
        return carry
    lax.fori_loop(0, 4, score, 0)
    for k in range(1, 4):
        g = (f + k) % 4
        send(tpart.at[:, at(g * 128, 128)], trecv.at[f], dev(f=g), r_t.at[f])
    total = tpart[:, at(f * 128, 128)].astype(F32)
    for k in range(1, 4):
        g = (f + k) % 4
        arrived(trecv.at[g], r_t.at[g])
        total = total + trecv[g].astype(F32)
    tall[s] = total.astype(BF16)

    load_z.wait()
    for n in range(4):
        part = wz.at[pl.ds(n * 32, 32)]
        arrived(part, r_w0.at[n], s > 0)
        send(part, part, dev(s=2), r_w0.at[n], s == 3)
    for j in range(3):
        def cross(j=j):
            if j > 0:
                arrived(wz.at[pl.ds(j * 128, 128)], r_w.at[j])
            upart[j] = dot(wz[j * 128:(j + 1) * 128], w[:, feats], 1, 1).astype(BF16)
        pl.when(j < s)(cross)
    some = s > 0
    for g, target in sixteen:
        send(upart.at[:, at(g % 4 * 32, 32), at(g // 4 * 128, 128)], urecv.at[group], target, r_u.at[group], some)

    for k in (3, 2, 1):
        send(tall.at[s], tall.at[s], dev(s=(s + k) % 4), r_ta.at[s], s + k < 4)

    def step(b, h):
        rows = pl.ds(h * 128, 128)
        need = b <= s

        def do():
            if h == 0:
                arrived(tall.at[b], r_ta.at[b], b < s)
            y = tall[b, rows].astype(F32)
            for j in range(b):
                y = y - dot(q[c, j, rows], u[b * (b - 1) // 2 + j].reshape(BLOCK, 128), 1, 0)
            q[c, b, rows, at(f * 128, 128)] = y.astype(BF16)
        pl.when(need)(do)
        mine = q.at[c, b, rows, at(f * 128, 128)]
        for k in range(1, 4):
            send(mine, mine, dev(f=(f + k) % 4), r_q.at[(b * 2 + h) * 4 + f], need)

    def complete(b, h):
        rows = pl.ds(h * 128, 128)
        need = b <= s
        for k in range(1, 4):
            g = (f + k) % 4
            arrived(q.at[c, b, rows, at(g * 128, 128)], r_q.at[(b * 2 + h) * 4 + g], need)
        send(q.at[c, b, rows], q.at[c, b, rows], dev(c=co), r_qc.at[b * 2 + h], need)

    step(0, 0)
    step(0, 1)

    def reduce_cross():
        total = upart[:, at(group % 4 * 32, 32), at(f * 128, 128)].astype(F32)
        for g, _ in sixteen:
            arrived(urecv.at[g], r_u.at[g])
            total = total + urecv[g].astype(F32)
        total = total.astype(BF16)
        for b in range(1, 4):
            def put(b=b):
                for j in range(b):
                    u[b * (b - 1) // 2 + j, xz, c] = total[j]
            pl.when(s == b)(put)
    pl.when(some)(reduce_cross)
    one, two, three = u.at[pl.ds(0, 1), xz, c], u.at[pl.ds(1, 2), xz, c], u.at[pl.ds(0, 6), xz, c]
    send(one, one, dev(s=3), r_us.at[0], s == 1)
    send(one, one, dev(s=2), r_us.at[0], s == 1)
    send(two, two, dev(s=3), r_us.at[1], s == 2)
    arrived(one, r_us.at[0], s >= 2)
    arrived(two, r_us.at[1], s == 3)
    for b in range(1, 4):
        n = b * (b + 1) // 2
        for p, target in planes:
            mine = u.at[pl.ds(0, n), xz, c]
            send(mine, mine, target, r_ux.at[xz], s == b)
        for p, _ in planes:
            arrived(u.at[pl.ds(0, n), p, c], r_ux.at[p], s == b)
        both = u.at[pl.ds(0, n), :, c]
        send(both, both, dev(c=co), r_uc, s == b)
        arrived(u.at[pl.ds(0, n), :, co], r_uc, s == b)

    for b in range(1, 5):
        for h in range(2):
            complete(b - 1, h)
            if b < 4:
                step(b, h)
    for b in range(4):
        for h in range(2):
            arrived(q.at[co, b, pl.ds(h * 128, 128)], r_qc.at[b * 2 + h], b <= s)
    proj[...] = q[c, s].astype(F32)

    for j in range(4):
        def gram(j=j):
            cols = at(f * 128, 128)
            g = dot(q[0, j], q[0, s, :, cols], 0, 0) + dot(q[1, j], q[1, s, :, cols], 0, 0)
            gpart[j] = g.astype(BF16).reshape(8, 2, 32, 128)
        pl.when(j <= s)(gram)

        def none(j=j):
            gpart[j] = jnp.zeros((8, 2, 32, 128), BF16)
        pl.when(j > s)(none)
    for p, target in planes:
        send(gpart.at[:, p, c], grecv.at[xz], target, r_g.at[xz])

    arrived(tok_other, r_tok)
    turned = [q[k, s].T for k in range(2)]
    mine_q = jnp.where(c == 0, turned[0], turned[1])
    other_q = jnp.where(c == 0, turned[1], turned[0])

    def hebb(t, half):
        here = dot(mine_q, tok[:, at(c * 2048 + half * 1024 + t * 256, 256)], 1, 0)
        there = dot(other_q, tok_other[:, at(half * 1024 + t * 256, 256)], 1, 0)
        return here + there

    def first(t, carry):
        ahalf[:, at(t * 256, 256)] = hebb(t, zo).astype(BF16)
        return carry
    lax.fori_loop(0, 4, first, 0)
    send(ahalf.at[pl.ds(0, H)], az, dev(z=zo), r_az)
    for k in range(1, 4):
        g = (x + k) % 4
        send(ahalf.at[pl.ds(H, BLOCK - H), at(g * 256, 256)], xb.at[x], dev(x=g), r_xb.at[x])

    def second(t, carry):
        afull[:, at(t * 256, 256)] = hebb(t, z)
        return carry
    lax.fori_loop(0, 4, second, 0)

    total = gpart[:, xz, c].astype(F32)
    for p, _ in planes:
        arrived(grecv.at[p], r_g.at[p])
        total = total + grecv[p].astype(F32)
    shape = (4, 32, 128)
    block = lax.broadcasted_iota(jnp.int32, shape, 0)
    col = d * 32 + lax.broadcasted_iota(jnp.int32, shape, 1)
    row = f * 128 + lax.broadcasted_iota(jnp.int32, shape, 2)
    keep = (block < s) | ((block == s) & (col <= row))
    gfull[:, at(group % 4 * 32, 32), at(f * 128, 128)] = jnp.where(keep, total, 0.0).astype(BF16)
    mine = gfull.at[:, at(group % 4 * 32, 32), at(f * 128, 128)]
    for g, target in sixteen:
        send(mine, mine, target, r_ga.at[group])
    for g, _ in sixteen:
        arrived(gfull.at[:, at(g % 4 * 32, 32), at(g // 4 * 128, 128)], r_ga.at[g])
    lower = gfull[...].reshape(512, BLOCK).T

    def damp(t, carry):
        cols = at(t * 256, 256)
        afull[:, cols] = afull[:, cols] - dot(lower, wz[:, cols], 1, 0)
        return carry
    lax.fori_loop(0, 4, damp, 0)

    mycols = at(x * 256, 256)
    p2[...] = afull[H:].astype(BF16)
    for k in range(1, 4):
        g = (x + k) % 4
        send(p2.at[:, at(g * 256, 256)], xc.at[x], dev(x=g), r_xc.at[x])
    arrived(az, r_az)
    afull[:H] = afull[:H] + az[...].astype(F32)
    s1[...] = afull[:H].astype(BF16)
    for k in range(1, 4):
        g = (x + k) % 4
        send(s1.at[:, at(g * 256, 256)], xa.at[x], dev(x=g), r_xa.at[x])
    total = ahalf[H:, mycols].astype(F32)
    for k in range(1, 4):
        g = (x + k) % 4
        arrived(xb.at[g], r_xb.at[g])
        total = total + xb[g].astype(F32)
    e2[...] = total.astype(BF16)
    send(e2, zb, dev(z=zo), r_zb)
    total = afull[H:, mycols]
    for k in range(1, 4):
        g = (x + k) % 4
        arrived(xc.at[g], r_xc.at[g])
        total = total + xc[g].astype(F32)
    arrived(zb, r_zb)
    total = total + zb[...].astype(F32)

    def cols_of(x, z, n=256):
        return at(c * 2048 + z * 1024 + x * 256, n)

    out[H:, cols_of(x, z)] = (total * SCALE).astype(BF16)
    total = afull[:H, mycols]
    for k in range(1, 4):
        g = (x + k) % 4
        arrived(xa.at[g], r_xa.at[g])
        total = total + xa[g].astype(F32)
    out[:H, cols_of(x, z)] = (total * SCALE).astype(BF16)

    right, left, far = (x + 1) % 4, (x + 3) % 4, (x + 2) % 4
    top, low = (0, TOP), (TOP, BLOCK - TOP)
    kinds = ((top, z), (low, z), (low, zo))
    cores = []

    def piece(rows, gx, gz, half=None, gc=c):
        start, size = rows
        if half is not None:
            start, size = start + half * (size // 2), size // 2
        return out.at[pl.ds(start, size), at(gc * 2048 + gz * 1024 + gx * 256, 256)]

    def to_core(rows, gx, gz, half=None):
        ref = piece(rows, gx, gz, half)
        send(ref, ref, dev(c=co), r_oc.at[len(cores)])
        cores.append((rows, gx, gz, half))

    def round_x(i):
        ref = piece(kinds[i][0], x, kinds[i][1])
        send(ref, ref, dev(x=right), r_ox.at[i * 4])
        send(ref, ref, dev(x=left), r_ox.at[i * 4 + 1])

    def pass_on(i):
        rows, gz = kinds[i]
        for g, half, to, n in ((left, 0, right, 0), (right, 1, left, 1)):
            arrived(piece(rows, g, gz), r_ox.at[i * 4 + n])
            ref = piece(rows, g, gz, half)
            send(ref, ref, dev(x=to), r_ox.at[i * 4 + 2 + n])
            if i == 0:
                over_z(g)
            to_core(rows, g, gz)

    def last(i):
        rows, gz = kinds[i]
        for half in range(2):
            arrived(piece(rows, far, gz, half), r_ox.at[i * 4 + 2 + half])
            if i == 0:
                over_z(far, half)
            to_core(rows, far, gz, half)

    overs = []

    def over_z(g, half=None):
        ref = piece(top, g, z, half)
        send(ref, ref, dev(z=zo), r_oz.at[len(overs)])
        overs.append((g, half))

    mine = piece(low, x, z)
    send(mine, mine, dev(z=zo), r_oz.at[5])
    round_x(1)
    round_x(0)
    over_z(x)
    to_core(low, x, z)
    to_core(top, x, z)
    arrived(piece(low, x, zo), r_oz.at[5])
    round_x(2)
    to_core(low, x, zo)
    pass_on(0)
    pass_on(1)
    pass_on(2)
    last(0)
    last(1)
    last(2)
    for n, (g, half) in enumerate(overs):
        arrived(piece(top, g, zo, half), r_oz.at[n])
        to_core(top, g, zo, half)
    for n, (rows, gx, gz, half) in enumerate(cores):
        arrived(piece(rows, gx, gz, half, co), r_oc.at[n])
    for copy, cond in pending:
        when(cond, copy.wait_send)


def shards(tokens, basis):
    dma = pltpu.SemaphoreType.DMA
    vm = pltpu.VMEM
    out, proj = pl.pallas_call(
        kernel,
        out_shape=(
            pltpu.VMEM((BLOCK, WIDTH), BF16),
            pltpu.VMEM((ROWS, BLOCK), F32),
        ),
        in_specs=[pl.BlockSpec(memory_space=pl.ANY)] * 2,
        out_specs=(pl.BlockSpec(memory_space=pltpu.VMEM), pl.BlockSpec(memory_space=pltpu.VMEM)),
        scratch_shapes=[
            vm((ROWS, WIDTH), BF16),
            vm((ROWS, 2048), BF16),
            vm((BLOCK, WIDTH), BF16),
            vm((512, 1024), BF16),
            vm((ROWS, BLOCK), BF16),
            vm((4, ROWS, 128), BF16),
            vm((4, ROWS, 128), BF16),
            vm((3, 128, 512), BF16),
            vm((16, 3, 32, 128), BF16),
            vm((6, 8, 2, 32, 128), BF16),
            vm((2, 4, ROWS, BLOCK), BF16),
            vm((4, 8, 2, 32, 128), BF16),
            vm((8, 4, 32, 128), BF16),
            vm((4, 128, 512), BF16),
            vm((BLOCK, 1024), BF16),
            vm((BLOCK, 1024), F32),
            vm((H, 1024), BF16),
            vm((H, 1024), BF16),
            vm((BLOCK - H, 1024), BF16),
            vm((4, H, 256), BF16),
            vm((4, BLOCK - H, 256), BF16),
            vm((4, BLOCK - H, 256), BF16),
            vm((BLOCK - H, 256), BF16),
            vm((BLOCK - H, 256), BF16),
            dma((220,)),
            dma((3,)),
            dma,
            dma((4,)),
            dma((4,)),
            dma((4,)),
            dma((16,)),
            dma((2,)),
            dma((8,)),
            dma,
            dma((32,)),
            dma((8,)),
            dma((8,)),
            dma((16,)),
            dma,
            dma((4,)),
            dma((4,)),
            dma((4,)),
            dma,
            dma((12,)),
            dma((6,)),
            dma((24,)),
            dma((4,)),
        ],
        compiler_params=pltpu.CompilerParams(
            collective_id=0, has_side_effects=True, vmem_limit_bytes=56 << 20
        ),
        name="sanger",
    )(tokens, basis)
    return out, proj


def solution(mesh):
    in_specs = (P("dp", "feat"), P("section", "feat"))
    out_specs = (P("section", "feat"), P("dp", "section"))
    return jax.shard_map(shards, mesh=mesh, in_specs=in_specs, out_specs=out_specs, check_vma=False)
```

```python
import functools
import math

import jax
import jax.numpy as jnp
from jax import lax
from jax.experimental import pallas as pl
from jax.experimental.pallas import tpu as pltpu
from jax.sharding import PartitionSpec as P

D = 16384
BF16 = jnp.bfloat16
F32 = jnp.float32
MESH = pl.DeviceIdType.MESH
ROWS = 256
WIDTH = 4096
BLOCK = 512
PARTS = 2
PART = ROWS // PARTS
H = 64
TOP = 256
SCALE = math.sqrt(D) / 4096


def dot(a, b, ca, cb):
    return lax.dot_general(a, b, (((ca,), (cb,)), ((), ())), preferred_element_type=F32)


def at(start, size):
    return pl.ds(pl.multiple_of(start, size), size)


def kernel(
    tokens, basis, out, proj,
    tok, tok_other, w, wz, tpart, trecv, tall, upart, ucore, usum, urecv, u, q, gpart, grecv, gfull, turned,
    ahalf, afull, az, s1, p2, xa, oa, sa, xb, ob, sb, xc, oc, sc, e2, zb,
    ssem, lsem, r_tok, r_w, r_t, r_ta, r_u, r_us, r_ux, r_uc, r_q, r_qc, r_g, r_ga,
    r_az, r_xa, r_xb, r_xc, r_zb, r_ox, r_oz, r_oc, r_w0, r_uh, r_gc,
):
    s = lax.axis_index("section")
    d = lax.axis_index("dp")
    f = lax.axis_index("feat")
    x, z, c = d // 4, (d // 2) % 2, d % 2
    xz = d // 2
    zo, co = 1 - z, 1 - c

    def dev(s=s, x=x, z=z, c=c, f=f):
        return (s, x * 4 + z * 2 + c, f)

    pending = []
    bufs_a, bufs_b, bufs_c = (xa, oa, sa), (xb, ob, sb), (xc, oc, sc)

    def when(cond, do):
        if cond is None:
            do()
        else:
            pl.when(cond)(do)

    def send(src, dst, target, sem, cond=None):
        copy = pltpu.make_async_remote_copy(
            src_ref=src, dst_ref=dst, send_sem=ssem.at[len(pending)], recv_sem=sem,
            device_id=target, device_id_type=MESH,
        )
        when(cond, copy.start)
        pending.append((copy, cond))

    def arrived(dst, sem, cond=None):
        when(cond, pltpu.make_async_copy(dst, dst, sem).wait)

    feats = at((2 * c + z) * 1024, 1024)
    load_tok = pltpu.make_async_copy(tokens, tok, lsem.at[0])
    load_w = pltpu.make_async_copy(basis, w, lsem.at[1])
    load_z = pltpu.make_async_copy(basis.at[at(x * 128, 128), feats], wz.at[at(s * 128, 128)], lsem.at[2])
    load_tok.start()
    load_w.start()
    load_z.start()

    group = f * 4 + z * 2 + c
    sections = [dev(s=(s + k) % 4) for k in range(1, 4)]
    eight = []
    for k in range(1, 8):
        g = (f + k // 2) % 4 * 2 + (z + k) % 2
        eight.append((g, dev(f=g // 2, z=g % 2)))
    planes = []
    for k in range(1, 8):
        p = (xz // 2 + k // 2) % 4 * 2 + (z + k) % 2
        planes.append((p, dev(x=p // 2, z=p % 2)))
    barrier = pltpu.get_barrier_semaphore()
    friends = sections + [dev(c=co)] + [t for _, t in eight] + [t for k, (_, t) in enumerate(planes, 1) if k // 2 > 0]
    for target in friends:
        pl.semaphore_signal(barrier, inc=1, device_id=target, device_id_type=MESH)
    for j in range(3):
        def clear(j=j):
            upart[j] = jnp.zeros((2, 2, 32, 512), BF16)
        pl.when(j >= s)(clear)
    for j in range(1, 4):
        def clear(j=j):
            wz[j * 128:(j + 1) * 128] = jnp.zeros((128, 1024), BF16)
        pl.when(j > s)(clear)
    pl.semaphore_wait(barrier, len(friends))

    def slice_zero(n):
        for b in (3, 1):
            send(basis.at[at(x * 128 + n * 32, 32), feats], wz.at[pl.ds(n * 32, 32)], dev(s=b), r_w0.at[n], s == 0)

    def relay(n, cond):
        part = wz.at[pl.ds(n * 32, 32)]
        arrived(part, r_w0.at[n], cond)
        send(part, part, dev(s=2), r_w0.at[n], s == 3)

    slice_zero(0)
    def slice_on(k, cond):
        send(basis.at[at(x * 128, 128), feats], wz.at[at(s * 128, 128)], dev(s=(s + k) % 4), r_w.at[s], cond)

    slice_on(1, (s == 1) | (s == 2))
    load_tok.wait()
    send(tok.at[:, at(co * 2048, 2048)], tok_other, dev(c=co), r_tok)
    load_w.wait()

    def score(t, carry):
        cols = at(t * 128, 128)
        tpart[:, cols] = dot(tok[...], w[cols, :], 1, 1).astype(BF16)
        return carry
    lax.fori_loop(0, 4, score, 0)
    slice_zero(1)
    for k in range(1, 4):
        g = (f + k) % 4
        send(tpart.at[:, at(g * 128, 128)], trecv.at[f], dev(f=g), r_t.at[f])
    slice_zero(2)
    for n in range(2):
        relay(n, s == 3)
    total = tpart[:, at(f * 128, 128)].astype(F32)
    for k in range(1, 4):
        g = (f + k) % 4
        arrived(trecv.at[g], r_t.at[g])
        total = total + trecv[g].astype(F32)
    slice_zero(3)
    slice_on(2, s == 1)
    tall[s] = total.astype(BF16)

    load_z.wait()
    for n in range(2):
        arrived(wz.at[pl.ds(n * 32, 32)], r_w0.at[n], (s > 0) & (s < 3))
    for n in range(2, 4):
        relay(n, s > 0)
    for j in range(3):
        def cross(j=j):
            if j > 0:
                arrived(wz.at[pl.ds(j * 128, 128)], r_w.at[j])
            upart[j] = dot(wz[j * 128:(j + 1) * 128], w[:, feats], 1, 1).astype(BF16).reshape(2, 2, 32, 512)
        pl.when(j < s)(cross)
    some = s > 0
    send(upart.at[:, :, co], ucore, dev(c=co), r_uh, some)

    def add_core():
        arrived(ucore, r_uh)
        usum[...] = (upart[:, :, c].astype(F32) + ucore[...].astype(F32)).astype(BF16)
    pl.when(some)(add_core)
    for g, target in eight:
        send(usum.at[:, g % 2, :, at(g // 2 * 128, 128)], urecv.at[f * 2 + z], target, r_u.at[f * 2 + z], some)

    for k in (3, 2, 1):
        send(tall.at[s], tall.at[s], dev(s=(s + k) % 4), r_ta.at[s], s + k < 4)

    def step(b, h):
        rows = pl.ds(h * PART, PART)
        need = b <= s

        def do():
            if h == 0:
                arrived(tall.at[b], r_ta.at[b], b < s)
            y = tall[b, rows].astype(F32)
            for j in range(b):
                y = y - dot(q[c, j, rows], u[b * (b - 1) // 2 + j].reshape(BLOCK, 128), 1, 0)
            q[c, b, rows, at(f * 128, 128)] = y.astype(BF16)
        pl.when(need)(do)
        mine = q.at[c, b, rows, at(f * 128, 128)]
        for k in range(1, 4):
            send(mine, mine, dev(f=(f + k) % 4), r_q.at[(b * PARTS + h) * 4 + f], need)

    def complete(b, h):
        rows = pl.ds(h * PART, PART)
        need = b <= s
        for k in range(1, 4):
            g = (f + k) % 4
            arrived(q.at[c, b, rows, at(g * 128, 128)], r_q.at[(b * PARTS + h) * 4 + g], need)
        send(q.at[c, b, rows], q.at[c, b, rows], dev(c=co), r_qc.at[b * PARTS + h], need)

    def reduce_cross():
        total = usum[:, z, :, at(f * 128, 128)].astype(F32)
        for g, _ in eight:
            arrived(urecv.at[g], r_u.at[g])
            total = total + urecv[g].astype(F32)
        total = total.astype(BF16)
        for b in range(1, 4):
            def put(b=b):
                for j in range(b):
                    u[b * (b - 1) // 2 + j, xz, c] = total[j]
            pl.when(s == b)(put)
    pl.when(some)(reduce_cross)

    def column(k, of, gc=None):
        return u.at[pl.ds(k * (k - 1) // 2, k), of, c if gc is None else gc]

    def spread(k, cond):
        for _, target in planes:
            send(column(k, xz), column(k, xz), target, r_ux.at[k * 8 + xz], cond)

    def to_core(k, cond):
        for p, _ in planes:
            arrived(column(k, p), r_ux.at[k * 8 + p], cond)
        both = column(k, slice(None))
        send(both, both, dev(c=co), r_uc.at[k], cond)

    def ready(k):
        arrived(column(k, slice(None), co), r_uc.at[k], s >= k)

    send(column(1, xz), column(1, xz), dev(s=3), r_us.at[1], s == 1)
    send(column(2, xz), column(2, xz), dev(s=3), r_us.at[2], s == 2)
    send(column(1, xz), column(1, xz), dev(s=2), r_us.at[1], s == 1)
    for k in range(1, 4):
        spread(k, s == k)
    arrived(column(1, xz), r_us.at[1], s >= 2)
    spread(1, s >= 2)
    for h in range(PARTS):
        step(0, h)
    to_core(1, s >= 1)
    for k in range(2, 4):
        to_core(k, s == k)
    for b in range(1, 5):
        if b == 2:
            arrived(column(2, xz), r_us.at[2], s == 3)
            spread(2, s == 3)
            to_core(2, s == 3)
        if b < 4:
            ready(b)
        for h in range(PARTS):
            complete(b - 1, h)
            if b < 4:
                step(b, h)
    for b in range(4):
        for h in range(PARTS):
            arrived(q.at[co, b, pl.ds(h * PART, PART)], r_qc.at[b * PARTS + h], b <= s)
    proj[...] = q[c, s].astype(F32)

    for k in range(2):
        turned[k] = q[k, s].T
    for j in range(4):
        def gram(j=j):
            rows = at(f * 128, 128)
            g = dot(turned[0, rows], q[0, j], 1, 0) + dot(turned[1, rows], q[1, j], 1, 0)
            gpart[j] = g.astype(BF16)
        pl.when(j <= s)(gram)

        def none(j=j):
            gpart[j] = jnp.zeros((128, BLOCK), BF16)
        pl.when(j > s)(none)
    for p, target in planes:
        mine = gpart.at[:, at((p % 2 * 2 + c) * 32, 32), at(p // 2 * 128, 128)]
        send(mine, grecv.at[xz], target, r_g.at[xz])

    mycols = at(x * 256, 256)
    arrived(tok_other, r_tok)

    def hebb(t, half):
        here = dot(turned[c], tok[:, at(c * 2048 + half * 1024 + t * 256, 256)], 1, 0)
        there = dot(turned[co], tok_other[:, at(half * 1024 + t * 256, 256)], 1, 0)
        return here + there

    right, left, far = (x + 1) % 4, (x + 3) % 4, (x + 2) % 4

    def block_of(ref, start, size, g):
        return ref.at[pl.ds(start, size), at(g * 256, 256)]

    def sum_start(src, start, size, bufs, sems):
        half = size // 2
        passing, sides = bufs[0], bufs[2]
        for to, n in ((right, 0), (left, 1)):
            send(block_of(src, start + n * half, half, far), passing.at[n], dev(x=to), sems.at[n])
        for to, n in ((right, 0), (left, 1)):
            m = 1 - n
            send(block_of(src, start + m * half, half, to), sides.at[n, pl.ds(m * half, half)], dev(x=to), sems.at[2 + n])

    def sum_pass(src, start, size, bufs, sems):
        half = size // 2
        passing, onward, sides = bufs
        for to, n in ((right, 0), (left, 1)):
            arrived(passing.at[n], sems.at[n])
            more = block_of(src, start + n * half, half, to)[...].astype(F32) + passing[n].astype(F32)
            onward[n] = more.astype(BF16)
            send(onward.at[n], sides.at[n, pl.ds(n * half, half)], dev(x=to), sems.at[4 + n])

    def sum_end(size, bufs, sems):
        half = size // 2
        sides = bufs[2]
        for n in range(2):
            arrived(sides.at[n, pl.ds((1 - n) * half, half)], sems.at[2 + n])
            arrived(sides.at[n, pl.ds(n * half, half)], sems.at[4 + n])
        return sides[0].astype(F32) + sides[1].astype(F32)

    def first(t, carry):
        ahalf[:, at(t * 256, 256)] = hebb(t, zo).astype(BF16)
        return carry
    lax.fori_loop(0, 4, first, 0)
    send(ahalf.at[pl.ds(0, H)], az, dev(z=zo), r_az)
    sum_start(ahalf, H, BLOCK - H, bufs_b, r_xb)

    total = gpart[:, at(group % 4 * 32, 32), at(x * 128, 128)].astype(F32)
    for p, _ in planes:
        arrived(grecv.at[p], r_g.at[p])
        total = total + grecv[p].astype(F32)
    shape = (4, 32, 128)
    block = lax.broadcasted_iota(jnp.int32, shape, 0)
    row = group * 32 + lax.broadcasted_iota(jnp.int32, shape, 1)
    col = x * 128 + lax.broadcasted_iota(jnp.int32, shape, 2)
    keep = (block < s) | ((block == s) & (col <= row))
    mine = gfull.at[:, at(group * 32, 32)]
    mine[...] = jnp.where(keep, total, 0.0).astype(BF16)
    for _, target in eight:
        send(mine, mine, target, r_ga.at[f * 2 + z])
    send(mine, mine, dev(c=co), r_gc.at[f * 2 + z])

    def second(t, carry):
        afull[:, at(t * 256, 256)] = hebb(t, z)
        return carry
    lax.fori_loop(0, 4, second, 0)

    sum_pass(ahalf, H, BLOCK - H, bufs_b, r_xb)
    for g, _ in eight:
        mine = gfull.at[:, at((g * 2 + c) * 32, 32)]
        arrived(mine, r_ga.at[g])
        send(mine, mine, dev(c=co), r_gc.at[g])
    for g in range(8):
        arrived(gfull.at[:, at((g * 2 + co) * 32, 32)], r_gc.at[g])

    def damp(start, size):
        rows = pl.ds(start, size)

        def tile(t, carry):
            cols = at(t * 256, 256)
            sums = afull[rows, cols]
            for j in range(4):
                sums = sums - dot(gfull[j, rows], wz[j * 128:(j + 1) * 128, cols], 1, 0)
            afull[rows, cols] = sums
            return carry
        lax.fori_loop(0, 4, tile, 0)

    damp(0, H)
    arrived(az, r_az)
    afull[:H] = afull[:H] + az[...].astype(F32)
    s1[...] = afull[:H].astype(BF16)
    sum_start(s1, 0, H, bufs_a, r_xa)
    e2[...] = (ahalf[H:, mycols].astype(F32) + sum_end(BLOCK - H, bufs_b, r_xb)).astype(BF16)
    send(e2, zb, dev(z=zo), r_zb)
    damp(H, BLOCK - H)
    p2[...] = afull[H:].astype(BF16)
    sum_pass(afull, 0, H, bufs_a, r_xa)
    sum_start(p2, 0, BLOCK - H, bufs_c, r_xc)

    def cols_of(x, z, n=256):
        return at(c * 2048 + z * 1024 + x * 256, n)

    total = afull[:H, mycols] + sum_end(H, bufs_a, r_xa)
    out[:H, cols_of(x, z)] = (total * SCALE).astype(BF16)

    sum_pass(afull, H, BLOCK - H, bufs_c, r_xc)
    arrived(zb, r_zb)
    total = afull[H:, mycols] + zb[...].astype(F32) + sum_end(BLOCK - H, bufs_c, r_xc)
    out[H:, cols_of(x, z)] = (total * SCALE).astype(BF16)
    top, low = (0, TOP), (TOP, BLOCK - TOP)
    kinds = ((top, z), (low, z), (low, zo))
    cores = []

    def piece(rows, gx, gz, half=None, gc=c):
        start, size = rows
        if half is not None:
            start, size = start + half * (size // 2), size // 2
        return out.at[pl.ds(start, size), at(gc * 2048 + gz * 1024 + gx * 256, 256)]

    def across(rows, gx, gz, half=None):
        ref = piece(rows, gx, gz, half)
        send(ref, ref, dev(c=co), r_oc.at[len(cores)])
        cores.append((rows, gx, gz, half))

    def round_x(i):
        ref = piece(kinds[i][0], x, kinds[i][1])
        send(ref, ref, dev(x=right), r_ox.at[i * 4])
        send(ref, ref, dev(x=left), r_ox.at[i * 4 + 1])

    def pass_on(i):
        rows, gz = kinds[i]
        for g, half, to, n in ((left, 0, right, 0), (right, 1, left, 1)):
            arrived(piece(rows, g, gz), r_ox.at[i * 4 + n])
            ref = piece(rows, g, gz, half)
            send(ref, ref, dev(x=to), r_ox.at[i * 4 + 2 + n])
            if i == 0:
                over_z(g)
            across(rows, g, gz)

    def last(i):
        rows, gz = kinds[i]
        for half in range(2):
            arrived(piece(rows, far, gz, half), r_ox.at[i * 4 + 2 + half])
            if i == 0:
                over_z(far, half)
            across(rows, far, gz, half)

    overs = []

    def over_z(g, half=None):
        ref = piece(top, g, z, half)
        send(ref, ref, dev(z=zo), r_oz.at[len(overs)])
        overs.append((g, half))

    mine = piece(low, x, z)
    send(mine, mine, dev(z=zo), r_oz.at[5])
    round_x(0)
    over_z(x)
    round_x(1)
    across(top, x, z)
    across(low, x, z)
    pass_on(0)
    arrived(piece(low, x, zo), r_oz.at[5])
    round_x(2)
    across(low, x, zo)
    pass_on(1)
    pass_on(2)
    last(0)
    last(1)
    last(2)
    for n, (g, half) in enumerate(overs):
        arrived(piece(top, g, zo, half), r_oz.at[n])
        across(top, g, zo, half)
    for n, (rows, gx, gz, half) in enumerate(cores):
        arrived(piece(rows, gx, gz, half, co), r_oc.at[n])
    for sent in pending:
        if sent is not None:
            when(sent[1], sent[0].wait_send)


def shards(tokens, basis):
    dma = pltpu.SemaphoreType.DMA
    vm = pltpu.VMEM
    out, proj = pl.pallas_call(
        kernel,
        out_shape=(
            pltpu.VMEM((BLOCK, WIDTH), BF16),
            pltpu.VMEM((ROWS, BLOCK), F32),
        ),
        in_specs=[pl.BlockSpec(memory_space=pl.ANY)] * 2,
        out_specs=(pl.BlockSpec(memory_space=pltpu.VMEM), pl.BlockSpec(memory_space=pltpu.VMEM)),
        scratch_shapes=[
            vm((ROWS, WIDTH), BF16),
            vm((ROWS, 2048), BF16),
            vm((BLOCK, WIDTH), BF16),
            vm((512, 1024), BF16),
            vm((ROWS, BLOCK), BF16),
            vm((4, ROWS, 128), BF16),
            vm((4, ROWS, 128), BF16),
            vm((3, 2, 2, 32, 512), BF16),
            vm((3, 2, 32, 512), BF16),
            vm((3, 2, 32, 512), BF16),
            vm((8, 3, 32, 128), BF16),
            vm((6, 8, 2, 32, 128), BF16),
            vm((2, 4, ROWS, BLOCK), BF16),
            vm((4, 128, BLOCK), BF16),
            vm((8, 4, 32, 128), BF16),
            vm((4, BLOCK, 128), BF16),
            vm((2, BLOCK, ROWS), BF16),
            vm((BLOCK, 1024), BF16),
            vm((BLOCK, 1024), F32),
            vm((H, 1024), BF16),
            vm((H, 1024), BF16),
            vm((BLOCK - H, 1024), BF16),
            vm((2, H // 2, 256), BF16),
            vm((2, H // 2, 256), BF16),
            vm((2, H, 256), BF16),
            vm((2, (BLOCK - H) // 2, 256), BF16),
            vm((2, (BLOCK - H) // 2, 256), BF16),
            vm((2, BLOCK - H, 256), BF16),
            vm((2, (BLOCK - H) // 2, 256), BF16),
            vm((2, (BLOCK - H) // 2, 256), BF16),
            vm((2, BLOCK - H, 256), BF16),
            vm((BLOCK - H, 256), BF16),
            vm((BLOCK - H, 256), BF16),
            dma((300,)),
            dma((3,)),
            dma,
            dma((4,)),
            dma((4,)),
            dma((4,)),
            dma((16,)),
            dma((4,)),
            dma((32,)),
            dma((4,)),
            dma((16 * PARTS,)),
            dma((4 * PARTS,)),
            dma((8,)),
            dma((16,)),
            dma,
            dma((6,)),
            dma((6,)),
            dma((6,)),
            dma,
            dma((12,)),
            dma((6,)),
            dma((24,)),
            dma((4,)),
            dma,
            dma((8,)),
        ],
        compiler_params=pltpu.CompilerParams(
            collective_id=0, has_side_effects=True, vmem_limit_bytes=56 << 20
        ),
        name="sanger",
    )(tokens, basis)
    return out, proj


def solution(mesh):
    in_specs = (P("dp", "feat"), P("section", "feat"))
    out_specs = (P("section", "feat"), P("dp", "section"))
    return jax.shard_map(shards, mesh=mesh, in_specs=in_specs, out_specs=out_specs, check_vma=False)
```

```python
import functools
import math

import jax
import jax.numpy as jnp
from jax import lax
from jax.experimental import pallas as pl
from jax.experimental.pallas import tpu as pltpu
from jax.sharding import PartitionSpec as P

D = 16384
BF16 = jnp.bfloat16
F32 = jnp.float32
MESH = pl.DeviceIdType.MESH
ROWS = 256
WIDTH = 4096
BLOCK = 512
PARTS = 2
PART = ROWS // PARTS
H = 64
TOP = 256
SCALE = math.sqrt(D) / 4096


def dot(a, b, ca, cb):
    return lax.dot_general(a, b, (((ca,), (cb,)), ((), ())), preferred_element_type=F32)


def at(start, size):
    return pl.ds(pl.multiple_of(start, size), size)


def kernel(
    tokens, basis, out, proj,
    tok, tok_other, w, wz, tpart, trecv, tall, upart, ucore, usum, urecv, u, q, gpart, grecv, gfull, turned,
    ahalf, afull, az, s1, p2, xa, oa, sa, xb, ob, sb, xc, oc, sc, e2, zb,
    ssem, lsem, r_tok, r_w, r_t, r_ta, r_u, r_us, r_ux, r_uc, r_q, r_qc, r_g, r_ga,
    r_az, r_xa, r_xb, r_xc, r_zb, r_ox, r_oz, r_oc, r_w0, r_uh, r_gc,
):
    s = lax.axis_index("section")
    d = lax.axis_index("dp")
    f = lax.axis_index("feat")
    x, z, c = d // 4, (d // 2) % 2, d % 2
    xz = d // 2
    zo, co = 1 - z, 1 - c

    def dev(s=s, x=x, z=z, c=c, f=f):
        return (s, x * 4 + z * 2 + c, f)

    pending = []
    bufs_a, bufs_b, bufs_c = (xa, oa, sa), (xb, ob, sb), (xc, oc, sc)

    def when(cond, do):
        if cond is None:
            do()
        else:
            pl.when(cond)(do)

    def send(src, dst, target, sem, cond=None):
        copy = pltpu.make_async_remote_copy(
            src_ref=src, dst_ref=dst, send_sem=ssem.at[len(pending)], recv_sem=sem,
            device_id=target, device_id_type=MESH,
        )
        when(cond, copy.start)
        pending.append((copy, cond))

    def arrived(dst, sem, cond=None):
        when(cond, pltpu.make_async_copy(dst, dst, sem).wait)

    feats = at((2 * c + z) * 1024, 1024)
    load_tok = pltpu.make_async_copy(tokens, tok, lsem.at[0])
    load_w = pltpu.make_async_copy(basis, w, lsem.at[1])
    load_z = pltpu.make_async_copy(basis.at[at(x * 128, 128), feats], wz.at[at(s * 128, 128)], lsem.at[2])
    load_tok.start()
    load_w.start()
    load_z.start()

    group = f * 4 + z * 2 + c
    sections = [dev(s=(s + k) % 4) for k in range(1, 4)]
    eight = []
    for k in range(1, 8):
        g = (f + k // 2) % 4 * 2 + (z + k) % 2
        eight.append((g, dev(f=g // 2, z=g % 2)))
    planes = []
    for k in range(1, 8):
        p = (xz // 2 + k // 2) % 4 * 2 + (z + k) % 2
        planes.append((p, dev(x=p // 2, z=p % 2)))
    barrier = pltpu.get_barrier_semaphore()
    friends = sections + [dev(c=co)] + [t for _, t in eight] + [t for k, (_, t) in enumerate(planes, 1) if k // 2 > 0]
    for target in friends:
        pl.semaphore_signal(barrier, inc=1, device_id=target, device_id_type=MESH)
    for j in range(3):
        def clear(j=j):
            upart[j] = jnp.zeros((2, 2, 32, 512), BF16)
        pl.when(j >= s)(clear)
    for j in range(1, 4):
        def clear(j=j):
            wz[j * 128:(j + 1) * 128] = jnp.zeros((128, 1024), BF16)
        pl.when(j > s)(clear)
    pl.semaphore_wait(barrier, len(friends))

    def slice_zero(n):
        for b in (3, 1):
            send(basis.at[at(x * 128 + n * 32, 32), feats], wz.at[pl.ds(n * 32, 32)], dev(s=b), r_w0.at[n], s == 0)

    def relay(n, cond):
        part = wz.at[pl.ds(n * 32, 32)]
        arrived(part, r_w0.at[n], cond)
        send(part, part, dev(s=2), r_w0.at[n], s == 3)

    slice_zero(0)
    def slice_on(k, cond):
        send(basis.at[at(x * 128, 128), feats], wz.at[at(s * 128, 128)], dev(s=(s + k) % 4), r_w.at[s], cond)

    slice_on(1, (s == 1) | (s == 2))
    load_tok.wait()
    send(tok.at[:, at(co * 2048, 2048)], tok_other, dev(c=co), r_tok)
    load_w.wait()

    def score(t, carry):
        cols = at(t * 128, 128)
        tpart[:, cols] = dot(tok[...], w[cols, :], 1, 1).astype(BF16)
        return carry
    lax.fori_loop(0, 4, score, 0)
    slice_zero(1)
    for k in range(1, 4):
        g = (f + k) % 4
        send(tpart.at[:, at(g * 128, 128)], trecv.at[f], dev(f=g), r_t.at[f])
    slice_zero(2)
    for n in range(2):
        relay(n, s == 3)
    total = tpart[:, at(f * 128, 128)].astype(F32)
    for k in range(1, 4):
        g = (f + k) % 4
        arrived(trecv.at[g], r_t.at[g])
        total = total + trecv[g].astype(F32)
    slice_zero(3)
    slice_on(2, s == 1)
    tall[s] = total.astype(BF16)

    load_z.wait()
    for n in range(2):
        arrived(wz.at[pl.ds(n * 32, 32)], r_w0.at[n], (s > 0) & (s < 3))
    for n in range(2, 4):
        relay(n, s > 0)
    for j in range(3):
        def cross(j=j):
            if j > 0:
                arrived(wz.at[pl.ds(j * 128, 128)], r_w.at[j])
            upart[j] = dot(wz[j * 128:(j + 1) * 128], w[:, feats], 1, 1).astype(BF16).reshape(2, 2, 32, 512)
        pl.when(j < s)(cross)
    some = s > 0
    send(upart.at[:, :, co], ucore, dev(c=co), r_uh, some)

    def add_core():
        arrived(ucore, r_uh)
        usum[...] = (upart[:, :, c].astype(F32) + ucore[...].astype(F32)).astype(BF16)
    pl.when(some)(add_core)
    for g, target in eight:
        send(usum.at[:, g % 2, :, at(g // 2 * 128, 128)], urecv.at[f * 2 + z], target, r_u.at[f * 2 + z], some)

    for k in (3, 2, 1):
        send(tall.at[s], tall.at[s], dev(s=(s + k) % 4), r_ta.at[s], s + k < 4)

    def step(b, h):
        rows = pl.ds(h * PART, PART)
        need = b <= s

        def do():
            if h == 0:
                arrived(tall.at[b], r_ta.at[b], b < s)
            y = tall[b, rows].astype(F32)
            for j in range(b):
                y = y - dot(q[c, j, rows], u[b * (b - 1) // 2 + j].reshape(BLOCK, 128), 1, 0)
            q[c, b, rows, at(f * 128, 128)] = y.astype(BF16)
        pl.when(need)(do)
        mine = q.at[c, b, rows, at(f * 128, 128)]
        for k in range(1, 4):
            send(mine, mine, dev(f=(f + k) % 4), r_q.at[(b * PARTS + h) * 4 + f], need)

    def complete(b, h):
        rows = pl.ds(h * PART, PART)
        need = b <= s
        for k in range(1, 4):
            g = (f + k) % 4
            arrived(q.at[c, b, rows, at(g * 128, 128)], r_q.at[(b * PARTS + h) * 4 + g], need)
        send(q.at[c, b, rows], q.at[c, b, rows], dev(c=co), r_qc.at[b * PARTS + h], need)

    def reduce_cross():
        total = usum[:, z, :, at(f * 128, 128)].astype(F32)
        for g, _ in eight:
            arrived(urecv.at[g], r_u.at[g])
            total = total + urecv[g].astype(F32)
        total = total.astype(BF16)
        for b in range(1, 4):
            def put(b=b):
                for j in range(b):
                    u[b * (b - 1) // 2 + j, xz, c] = total[j]
            pl.when(s == b)(put)
    pl.when(some)(reduce_cross)

    def column(k, of, gc=None):
        return u.at[pl.ds(k * (k - 1) // 2, k), of, c if gc is None else gc]

    def spread(k, cond):
        for _, target in planes:
            send(column(k, xz), column(k, xz), target, r_ux.at[k * 8 + xz], cond)

    def to_core(k, cond):
        for p, _ in planes:
            arrived(column(k, p), r_ux.at[k * 8 + p], cond)
        both = column(k, slice(None))
        send(both, both, dev(c=co), r_uc.at[k], cond)

    def ready(k):
        arrived(column(k, slice(None), co), r_uc.at[k], s >= k)

    send(column(1, xz), column(1, xz), dev(s=3), r_us.at[1], s == 1)
    send(column(2, xz), column(2, xz), dev(s=3), r_us.at[2], s == 2)
    send(column(1, xz), column(1, xz), dev(s=2), r_us.at[1], s == 1)
    for k in range(1, 4):
        spread(k, s == k)
    arrived(column(1, xz), r_us.at[1], s >= 2)
    spread(1, s >= 2)
    for h in range(PARTS):
        step(0, h)
    to_core(1, s >= 1)
    for k in range(2, 4):
        to_core(k, s == k)
    for b in range(1, 5):
        if b == 2:
            arrived(column(2, xz), r_us.at[2], s == 3)
            spread(2, s == 3)
            to_core(2, s == 3)
        if b < 4:
            ready(b)
        for h in range(PARTS):
            complete(b - 1, h)
            if b < 4:
                step(b, h)
    for b in range(4):
        for h in range(PARTS):
            arrived(q.at[co, b, pl.ds(h * PART, PART)], r_qc.at[b * PARTS + h], b <= s)
    proj[...] = q[c, s].astype(F32)

    for k in range(2):
        turned[k] = q[k, s].T
    for j in range(4):
        def gram(j=j):
            rows = at(f * 128, 128)
            g = dot(turned[0, rows], q[0, j], 1, 0) + dot(turned[1, rows], q[1, j], 1, 0)
            gpart[j] = g.astype(BF16)
        pl.when(j <= s)(gram)

        def none(j=j):
            gpart[j] = jnp.zeros((128, BLOCK), BF16)
        pl.when(j > s)(none)
    for p, target in planes:
        mine = gpart.at[:, at((p % 2 * 2 + c) * 32, 32), at(p // 2 * 128, 128)]
        send(mine, grecv.at[xz], target, r_g.at[xz])

    mycols = at(x * 256, 256)
    arrived(tok_other, r_tok)

    def hebb(t, half):
        here = dot(turned[c], tok[:, at(c * 2048 + half * 1024 + t * 256, 256)], 1, 0)
        there = dot(turned[co], tok_other[:, at(half * 1024 + t * 256, 256)], 1, 0)
        return here + there

    right, left, far = (x + 1) % 4, (x + 3) % 4, (x + 2) % 4

    def block_of(ref, start, size, g):
        return ref.at[pl.ds(start, size), at(g * 256, 256)]

    def sum_start(src, start, size, bufs, sems):
        half = size // 2
        passing, sides = bufs[0], bufs[2]
        for to, n in ((right, 0), (left, 1)):
            send(block_of(src, start + n * half, half, far), passing.at[n], dev(x=to), sems.at[n])
        for to, n in ((right, 0), (left, 1)):
            m = 1 - n
            send(block_of(src, start + m * half, half, to), sides.at[n, pl.ds(m * half, half)], dev(x=to), sems.at[2 + n])

    def sum_pass(src, start, size, bufs, sems):
        half = size // 2
        passing, onward, sides = bufs
        for to, n in ((right, 0), (left, 1)):
            arrived(passing.at[n], sems.at[n])
            more = block_of(src, start + n * half, half, to)[...].astype(F32) + passing[n].astype(F32)
            onward[n] = more.astype(BF16)
            send(onward.at[n], sides.at[n, pl.ds(n * half, half)], dev(x=to), sems.at[4 + n])

    def sum_end(size, bufs, sems):
        half = size // 2
        sides = bufs[2]
        for n in range(2):
            arrived(sides.at[n, pl.ds((1 - n) * half, half)], sems.at[2 + n])
            arrived(sides.at[n, pl.ds(n * half, half)], sems.at[4 + n])
        return sides[0].astype(F32) + sides[1].astype(F32)

    def first(t, carry):
        ahalf[:, at(t * 256, 256)] = hebb(t, zo).astype(BF16)
        return carry
    lax.fori_loop(0, 4, first, 0)
    send(ahalf.at[pl.ds(0, H)], az, dev(z=zo), r_az)
    sum_start(ahalf, H, BLOCK - H, bufs_b, r_xb)

    total = gpart[:, at(group % 4 * 32, 32), at(x * 128, 128)].astype(F32)
    for p, _ in planes:
        arrived(grecv.at[p], r_g.at[p])
        total = total + grecv[p].astype(F32)
    shape = (4, 32, 128)
    block = lax.broadcasted_iota(jnp.int32, shape, 0)
    row = group * 32 + lax.broadcasted_iota(jnp.int32, shape, 1)
    col = x * 128 + lax.broadcasted_iota(jnp.int32, shape, 2)
    keep = (block < s) | ((block == s) & (col <= row))
    mine = gfull.at[:, at(group * 32, 32)]
    mine[...] = jnp.where(keep, total, 0.0).astype(BF16)
    for _, target in eight:
        send(mine, mine, target, r_ga.at[f * 2 + z])
    send(mine, mine, dev(c=co), r_gc.at[f * 2 + z])

    def second(t, carry):
        afull[:, at(t * 256, 256)] = hebb(t, z)
        return carry
    lax.fori_loop(0, 4, second, 0)

    sum_pass(ahalf, H, BLOCK - H, bufs_b, r_xb)
    for g, _ in eight:
        mine = gfull.at[:, at((g * 2 + c) * 32, 32)]
        arrived(mine, r_ga.at[g])
        send(mine, mine, dev(c=co), r_gc.at[g])
    for g in range(8):
        arrived(gfull.at[:, at((g * 2 + co) * 32, 32)], r_gc.at[g])

    def damp(start, size):
        rows = pl.ds(start, size)

        def tile(t, carry):
            cols = at(t * 256, 256)
            sums = afull[rows, cols]
            for j in range(4):
                sums = sums - dot(gfull[j, rows], wz[j * 128:(j + 1) * 128, cols], 1, 0)
            afull[rows, cols] = sums
            return carry
        lax.fori_loop(0, 4, tile, 0)

    damp(0, H)
    arrived(az, r_az)
    afull[:H] = afull[:H] + az[...].astype(F32)
    s1[...] = afull[:H].astype(BF16)
    sum_start(s1, 0, H, bufs_a, r_xa)
    damp(H, BLOCK - H)
    p2[...] = afull[H:].astype(BF16)
    sum_start(p2, 0, BLOCK - H, bufs_c, r_xc)
    e2[...] = (ahalf[H:, mycols].astype(F32) + sum_end(BLOCK - H, bufs_b, r_xb)).astype(BF16)
    send(e2, zb, dev(z=zo), r_zb)
    sum_pass(afull, 0, H, bufs_a, r_xa)
    sum_pass(afull, H, BLOCK - H, bufs_c, r_xc)

    def cols_of(x, z, n=256):
        return at(c * 2048 + z * 1024 + x * 256, n)

    total = afull[:H, mycols] + sum_end(H, bufs_a, r_xa)
    out[:H, cols_of(x, z)] = (total * SCALE).astype(BF16)

    arrived(zb, r_zb)
    total = afull[H:, mycols] + zb[...].astype(F32) + sum_end(BLOCK - H, bufs_c, r_xc)
    out[H:, cols_of(x, z)] = (total * SCALE).astype(BF16)
    top, low = (0, TOP), (TOP, BLOCK - TOP)
    kinds = ((top, z), (low, z), (low, zo))
    cores = []

    def piece(rows, gx, gz, half=None, gc=c):
        start, size = rows
        if half is not None:
            start, size = start + half * (size // 2), size // 2
        return out.at[pl.ds(start, size), at(gc * 2048 + gz * 1024 + gx * 256, 256)]

    def across(rows, gx, gz, half=None):
        ref = piece(rows, gx, gz, half)
        send(ref, ref, dev(c=co), r_oc.at[len(cores)])
        cores.append((rows, gx, gz, half))

    def round_x(i):
        ref = piece(kinds[i][0], x, kinds[i][1])
        send(ref, ref, dev(x=right), r_ox.at[i * 4])
        send(ref, ref, dev(x=left), r_ox.at[i * 4 + 1])

    def pass_on(i):
        rows, gz = kinds[i]
        for g, half, to, n in ((left, 0, right, 0), (right, 1, left, 1)):
            arrived(piece(rows, g, gz), r_ox.at[i * 4 + n])
            ref = piece(rows, g, gz, half)
            send(ref, ref, dev(x=to), r_ox.at[i * 4 + 2 + n])
            if i == 0:
                over_z(g)
            across(rows, g, gz)

    def last(i):
        rows, gz = kinds[i]
        for half in range(2):
            arrived(piece(rows, far, gz, half), r_ox.at[i * 4 + 2 + half])
            if i == 0:
                over_z(far, half)
            across(rows, far, gz, half)

    overs = []

    def over_z(g, half=None):
        ref = piece(top, g, z, half)
        send(ref, ref, dev(z=zo), r_oz.at[len(overs)])
        overs.append((g, half))

    mine = piece(low, x, z)
    send(mine, mine, dev(z=zo), r_oz.at[5])
    round_x(0)
    over_z(x)
    round_x(1)
    across(top, x, z)
    across(low, x, z)
    pass_on(0)
    arrived(piece(low, x, zo), r_oz.at[5])
    round_x(2)
    across(low, x, zo)
    pass_on(1)
    pass_on(2)
    last(0)
    last(1)
    last(2)
    for n, (g, half) in enumerate(overs):
        arrived(piece(top, g, zo, half), r_oz.at[n])
        across(top, g, zo, half)
    for n, (rows, gx, gz, half) in enumerate(cores):
        arrived(piece(rows, gx, gz, half, co), r_oc.at[n])
    for sent in pending:
        if sent is not None:
            when(sent[1], sent[0].wait_send)


def shards(tokens, basis):
    dma = pltpu.SemaphoreType.DMA
    vm = pltpu.VMEM
    out, proj = pl.pallas_call(
        kernel,
        out_shape=(
            pltpu.VMEM((BLOCK, WIDTH), BF16),
            pltpu.VMEM((ROWS, BLOCK), F32),
        ),
        in_specs=[pl.BlockSpec(memory_space=pl.ANY)] * 2,
        out_specs=(pl.BlockSpec(memory_space=pltpu.VMEM), pl.BlockSpec(memory_space=pltpu.VMEM)),
        scratch_shapes=[
            vm((ROWS, WIDTH), BF16),
            vm((ROWS, 2048), BF16),
            vm((BLOCK, WIDTH), BF16),
            vm((512, 1024), BF16),
            vm((ROWS, BLOCK), BF16),
            vm((4, ROWS, 128), BF16),
            vm((4, ROWS, 128), BF16),
            vm((3, 2, 2, 32, 512), BF16),
            vm((3, 2, 32, 512), BF16),
            vm((3, 2, 32, 512), BF16),
            vm((8, 3, 32, 128), BF16),
            vm((6, 8, 2, 32, 128), BF16),
            vm((2, 4, ROWS, BLOCK), BF16),
            vm((4, 128, BLOCK), BF16),
            vm((8, 4, 32, 128), BF16),
            vm((4, BLOCK, 128), BF16),
            vm((2, BLOCK, ROWS), BF16),
            vm((BLOCK, 1024), BF16),
            vm((BLOCK, 1024), F32),
            vm((H, 1024), BF16),
            vm((H, 1024), BF16),
            vm((BLOCK - H, 1024), BF16),
            vm((2, H // 2, 256), BF16),
            vm((2, H // 2, 256), BF16),
            vm((2, H, 256), BF16),
            vm((2, (BLOCK - H) // 2, 256), BF16),
            vm((2, (BLOCK - H) // 2, 256), BF16),
            vm((2, BLOCK - H, 256), BF16),
            vm((2, (BLOCK - H) // 2, 256), BF16),
            vm((2, (BLOCK - H) // 2, 256), BF16),
            vm((2, BLOCK - H, 256), BF16),
            vm((BLOCK - H, 256), BF16),
            vm((BLOCK - H, 256), BF16),
            dma((300,)),
            dma((3,)),
            dma,
            dma((4,)),
            dma((4,)),
            dma((4,)),
            dma((16,)),
            dma((4,)),
            dma((32,)),
            dma((4,)),
            dma((16 * PARTS,)),
            dma((4 * PARTS,)),
            dma((8,)),
            dma((16,)),
            dma,
            dma((6,)),
            dma((6,)),
            dma((6,)),
            dma,
            dma((12,)),
            dma((6,)),
            dma((24,)),
            dma((4,)),
            dma,
            dma((8,)),
        ],
        compiler_params=pltpu.CompilerParams(
            collective_id=0, has_side_effects=True, vmem_limit_bytes=56 << 20
        ),
        name="sanger",
    )(tokens, basis)
    return out, proj


def solution(mesh):
    in_specs = (P("dp", "feat"), P("section", "feat"))
    out_specs = (P("section", "feat"), P("dp", "section"))
    return jax.shard_map(shards, mesh=mesh, in_specs=in_specs, out_specs=out_specs, check_vma=False)
```

```python
import functools
import math

import jax
import jax.numpy as jnp
from jax import lax
from jax.experimental import pallas as pl
from jax.experimental.pallas import tpu as pltpu
from jax.sharding import PartitionSpec as P

D = 16384
BF16 = jnp.bfloat16
F32 = jnp.float32
MESH = pl.DeviceIdType.MESH
ROWS = 256
WIDTH = 4096
BLOCK = 512
PARTS = 2
PART = ROWS // PARTS
H = 64
TOP = 256
SCALE = math.sqrt(D) / 4096


def dot(a, b, ca, cb):
    return lax.dot_general(a, b, (((ca,), (cb,)), ((), ())), preferred_element_type=F32)


def at(start, size):
    return pl.ds(pl.multiple_of(start, size), size)


def kernel(
    tokens, basis, out, proj,
    tok, tok_other, w, wz, tpart, trecv, tall, upart, ucore, usum, urecv, u, q, gpart, grecv, gfull, turned,
    ahalf, afull, az, s1, p2, xa, oa, sa, xb, ob, sb, xc, oc, sc, e2, zb,
    ssem, lsem, r_tok, r_w, r_t, r_ta, r_u, r_us, r_ux, r_uc, r_q, r_qc, r_g, r_ga,
    r_az, r_xa, r_xb, r_xc, r_zb, r_ox, r_oz, r_oc, r_w0, r_uh, r_gc,
):
    s = lax.axis_index("section")
    d = lax.axis_index("dp")
    f = lax.axis_index("feat")
    x, z, c = d // 4, (d // 2) % 2, d % 2
    xz = d // 2
    zo, co = 1 - z, 1 - c

    def dev(s=s, x=x, z=z, c=c, f=f):
        return (s, x * 4 + z * 2 + c, f)

    pending = []
    bufs_a, bufs_b, bufs_c = (xa, oa, sa), (xb, ob, sb), (xc, oc, sc)

    def when(cond, do):
        if cond is None:
            do()
        else:
            pl.when(cond)(do)

    def send(src, dst, target, sem, cond=None):
        copy = pltpu.make_async_remote_copy(
            src_ref=src, dst_ref=dst, send_sem=ssem.at[len(pending)], recv_sem=sem,
            device_id=target, device_id_type=MESH,
        )
        when(cond, copy.start)
        pending.append((copy, cond))

    def arrived(dst, sem, cond=None):
        when(cond, pltpu.make_async_copy(dst, dst, sem).wait)

    feats = at((2 * c + z) * 1024, 1024)
    load_tok = pltpu.make_async_copy(tokens, tok, lsem.at[0])
    load_w = pltpu.make_async_copy(basis, w, lsem.at[1])
    load_z = pltpu.make_async_copy(basis.at[at(x * 128, 128), feats], wz.at[at(s * 128, 128)], lsem.at[2])
    load_tok.start()
    load_w.start()
    load_z.start()

    group = f * 4 + z * 2 + c
    sections = [dev(s=(s + k) % 4) for k in range(1, 4)]
    eight = []
    for k in range(1, 8):
        g = (f + k // 2) % 4 * 2 + (z + k) % 2
        eight.append((g, dev(f=g // 2, z=g % 2)))
    planes = []
    for k in range(1, 8):
        p = (xz // 2 + k // 2) % 4 * 2 + (z + k) % 2
        planes.append((p, dev(x=p // 2, z=p % 2)))
    barrier = pltpu.get_barrier_semaphore()
    friends = sections + [dev(c=co)] + [t for _, t in eight] + [t for k, (_, t) in enumerate(planes, 1) if k // 2 > 0]
    for target in friends:
        pl.semaphore_signal(barrier, inc=1, device_id=target, device_id_type=MESH)
    for j in range(3):
        def clear(j=j):
            upart[j] = jnp.zeros((2, 2, 32, 512), BF16)
        pl.when(j >= s)(clear)
    for j in range(1, 4):
        def clear(j=j):
            wz[j * 128:(j + 1) * 128] = jnp.zeros((128, 1024), BF16)
        pl.when(j > s)(clear)
    pl.semaphore_wait(barrier, len(friends))

    def slice_zero(n):
        for b in (3, 1):
            send(basis.at[at(x * 128 + n * 32, 32), feats], wz.at[pl.ds(n * 32, 32)], dev(s=b), r_w0.at[n], s == 0)

    def relay(n, cond):
        part = wz.at[pl.ds(n * 32, 32)]
        arrived(part, r_w0.at[n], cond)
        send(part, part, dev(s=2), r_w0.at[n], s == 3)

    slice_zero(0)
    def slice_on(k, cond):
        send(basis.at[at(x * 128, 128), feats], wz.at[at(s * 128, 128)], dev(s=(s + k) % 4), r_w.at[s], cond)

    slice_on(1, (s == 1) | (s == 2))
    load_tok.wait()
    send(tok.at[:, at(co * 2048, 2048)], tok_other, dev(c=co), r_tok)
    load_w.wait()

    def score(t, carry):
        cols = at(t * 128, 128)
        tpart[:, cols] = dot(tok[...], w[cols, :], 1, 1).astype(BF16)
        return carry
    lax.fori_loop(0, 4, score, 0)
    slice_zero(1)
    for k in range(1, 4):
        g = (f + k) % 4
        send(tpart.at[:, at(g * 128, 128)], trecv.at[f], dev(f=g), r_t.at[f])
    slice_zero(2)
    for n in range(2):
        relay(n, s == 3)
    total = tpart[:, at(f * 128, 128)].astype(F32)
    for k in range(1, 4):
        g = (f + k) % 4
        arrived(trecv.at[g], r_t.at[g])
        total = total + trecv[g].astype(F32)
    slice_zero(3)
    slice_on(2, s == 1)
    tall[s] = total.astype(BF16)

    load_z.wait()
    for n in range(2):
        arrived(wz.at[pl.ds(n * 32, 32)], r_w0.at[n], (s > 0) & (s < 3))
    for n in range(2, 4):
        relay(n, s > 0)
    for j in range(3):
        def cross(j=j):
            if j > 0:
                arrived(wz.at[pl.ds(j * 128, 128)], r_w.at[j])
            upart[j] = dot(wz[j * 128:(j + 1) * 128], w[:, feats], 1, 1).astype(BF16).reshape(2, 2, 32, 512)
        pl.when(j < s)(cross)
    some = s > 0
    send(upart.at[:, :, co], ucore, dev(c=co), r_uh, some)

    def add_core():
        arrived(ucore, r_uh)
        usum[...] = (upart[:, :, c].astype(F32) + ucore[...].astype(F32)).astype(BF16)
    pl.when(some)(add_core)
    for g, target in eight:
        send(usum.at[:, g % 2, :, at(g // 2 * 128, 128)], urecv.at[f * 2 + z], target, r_u.at[f * 2 + z], some)

    for k in (3, 2, 1):
        send(tall.at[s], tall.at[s], dev(s=(s + k) % 4), r_ta.at[s], s + k < 4)

    def step(b, h):
        rows = pl.ds(h * PART, PART)
        need = b <= s

        def do():
            if h == 0:
                arrived(tall.at[b], r_ta.at[b], b < s)
            y = tall[b, rows].astype(F32)
            for j in range(b):
                y = y - dot(q[c, j, rows], u[b * (b - 1) // 2 + j].reshape(BLOCK, 128), 1, 0)
            q[c, b, rows, at(f * 128, 128)] = y.astype(BF16)
        pl.when(need)(do)
        mine = q.at[c, b, rows, at(f * 128, 128)]
        for k in range(1, 4):
            send(mine, mine, dev(f=(f + k) % 4), r_q.at[(b * PARTS + h) * 4 + f], need)

    def complete(b, h):
        rows = pl.ds(h * PART, PART)
        need = b <= s
        for k in range(1, 4):
            g = (f + k) % 4
            arrived(q.at[c, b, rows, at(g * 128, 128)], r_q.at[(b * PARTS + h) * 4 + g], need)
        send(q.at[c, b, rows], q.at[c, b, rows], dev(c=co), r_qc.at[b * PARTS + h], need)

    def reduce_cross():
        total = usum[:, z, :, at(f * 128, 128)].astype(F32)
        for g, _ in eight:
            arrived(urecv.at[g], r_u.at[g])
            total = total + urecv[g].astype(F32)
        total = total.astype(BF16)
        for b in range(1, 4):
            def put(b=b):
                for j in range(b):
                    u[b * (b - 1) // 2 + j, xz, c] = total[j]
            pl.when(s == b)(put)
    pl.when(some)(reduce_cross)

    def column(k, of, gc=None):
        return u.at[pl.ds(k * (k - 1) // 2, k), of, c if gc is None else gc]

    def spread(k, cond):
        for _, target in planes:
            send(column(k, xz), column(k, xz), target, r_ux.at[k * 8 + xz], cond)

    def to_core(k, cond):
        for p, _ in planes:
            arrived(column(k, p), r_ux.at[k * 8 + p], cond)
        both = column(k, slice(None))
        send(both, both, dev(c=co), r_uc.at[k], cond)

    def ready(k):
        arrived(column(k, slice(None), co), r_uc.at[k], s >= k)

    send(column(1, xz), column(1, xz), dev(s=3), r_us.at[1], s == 1)
    send(column(2, xz), column(2, xz), dev(s=3), r_us.at[2], s == 2)
    send(column(1, xz), column(1, xz), dev(s=2), r_us.at[1], s == 1)
    arrived(column(1, xz), r_us.at[1], s >= 2)
    spread(1, s >= 2)
    for k in range(1, 4):
        spread(k, s == k)
    for h in range(PARTS):
        step(0, h)
    to_core(1, s >= 1)
    to_core(2, s == 2)
    for b in range(1, 5):
        if b == 2:
            arrived(column(2, xz), r_us.at[2], s == 3)
            spread(2, s == 3)
            to_core(3, s == 3)
            to_core(2, s == 3)
        if b < 4:
            ready(b)
        for h in range(PARTS):
            complete(b - 1, h)
            if b < 4:
                step(b, h)
    for b in range(4):
        for h in range(PARTS):
            arrived(q.at[co, b, pl.ds(h * PART, PART)], r_qc.at[b * PARTS + h], b <= s)
    proj[...] = q[c, s].astype(F32)

    for k in range(2):
        turned[k] = q[k, s].T
    for j in range(4):
        def gram(j=j):
            rows = at(f * 128, 128)
            g = dot(turned[0, rows], q[0, j], 1, 0) + dot(turned[1, rows], q[1, j], 1, 0)
            gpart[j] = g.astype(BF16)
        pl.when(j <= s)(gram)

        def none(j=j):
            gpart[j] = jnp.zeros((128, BLOCK), BF16)
        pl.when(j > s)(none)
    for p, target in planes:
        mine = gpart.at[:, at((p % 2 * 2 + c) * 32, 32), at(p // 2 * 128, 128)]
        send(mine, grecv.at[xz], target, r_g.at[xz])

    mycols = at(x * 256, 256)
    arrived(tok_other, r_tok)

    def hebb(t, half):
        here = dot(turned[c], tok[:, at(c * 2048 + half * 1024 + t * 256, 256)], 1, 0)
        there = dot(turned[co], tok_other[:, at(half * 1024 + t * 256, 256)], 1, 0)
        return here + there

    right, left, far = (x + 1) % 4, (x + 3) % 4, (x + 2) % 4

    def block_of(ref, start, size, g):
        return ref.at[pl.ds(start, size), at(g * 256, 256)]

    def sum_start(src, start, size, bufs, sems):
        half = size // 2
        passing, sides = bufs[0], bufs[2]
        for to, n in ((right, 0), (left, 1)):
            send(block_of(src, start + n * half, half, far), passing.at[n], dev(x=to), sems.at[n])
        for to, n in ((right, 0), (left, 1)):
            m = 1 - n
            send(block_of(src, start + m * half, half, to), sides.at[n, pl.ds(m * half, half)], dev(x=to), sems.at[2 + n])

    def sum_pass(src, start, size, bufs, sems):
        half = size // 2
        passing, onward, sides = bufs
        for to, n in ((right, 0), (left, 1)):
            arrived(passing.at[n], sems.at[n])
            more = block_of(src, start + n * half, half, to)[...].astype(F32) + passing[n].astype(F32)
            onward[n] = more.astype(BF16)
            send(onward.at[n], sides.at[n, pl.ds(n * half, half)], dev(x=to), sems.at[4 + n])

    def sum_end(size, bufs, sems):
        half = size // 2
        sides = bufs[2]
        for n in range(2):
            arrived(sides.at[n, pl.ds((1 - n) * half, half)], sems.at[2 + n])
            arrived(sides.at[n, pl.ds(n * half, half)], sems.at[4 + n])
        return sides[0].astype(F32) + sides[1].astype(F32)

    def first(t, carry):
        ahalf[:, at(t * 256, 256)] = hebb(t, zo).astype(BF16)
        return carry
    lax.fori_loop(0, 4, first, 0)
    send(ahalf.at[pl.ds(0, H)], az, dev(z=zo), r_az)
    sum_start(ahalf, H, BLOCK - H, bufs_b, r_xb)

    total = gpart[:, at(group % 4 * 32, 32), at(x * 128, 128)].astype(F32)
    for p, _ in planes:
        arrived(grecv.at[p], r_g.at[p])
        total = total + grecv[p].astype(F32)
    shape = (4, 32, 128)
    block = lax.broadcasted_iota(jnp.int32, shape, 0)
    row = group * 32 + lax.broadcasted_iota(jnp.int32, shape, 1)
    col = x * 128 + lax.broadcasted_iota(jnp.int32, shape, 2)
    keep = (block < s) | ((block == s) & (col <= row))
    mine = gfull.at[:, at(group * 32, 32)]
    mine[...] = jnp.where(keep, total, 0.0).astype(BF16)
    for _, target in eight:
        send(mine, mine, target, r_ga.at[f * 2 + z])
    send(mine, mine, dev(c=co), r_gc.at[f * 2 + z])

    def second(t, carry):
        afull[:, at(t * 256, 256)] = hebb(t, z)
        return carry
    lax.fori_loop(0, 4, second, 0)

    sum_pass(ahalf, H, BLOCK - H, bufs_b, r_xb)
    for g, _ in eight:
        mine = gfull.at[:, at((g * 2 + c) * 32, 32)]
        arrived(mine, r_ga.at[g])
        send(mine, mine, dev(c=co), r_gc.at[g])
    for g in range(8):
        arrived(gfull.at[:, at((g * 2 + co) * 32, 32)], r_gc.at[g])

    def damp(start, size):
        rows = pl.ds(start, size)

        def tile(t, carry):
            cols = at(t * 256, 256)
            sums = afull[rows, cols]
            for j in range(4):
                sums = sums - dot(gfull[j, rows], wz[j * 128:(j + 1) * 128, cols], 1, 0)
            afull[rows, cols] = sums
            return carry
        lax.fori_loop(0, 4, tile, 0)

    damp(0, H)
    arrived(az, r_az)
    afull[:H] = afull[:H] + az[...].astype(F32)
    s1[...] = afull[:H].astype(BF16)
    sum_start(s1, 0, H, bufs_a, r_xa)
    damp(H, BLOCK - H)
    p2[...] = afull[H:].astype(BF16)
    sum_start(p2, 0, BLOCK - H, bufs_c, r_xc)
    e2[...] = (ahalf[H:, mycols].astype(F32) + sum_end(BLOCK - H, bufs_b, r_xb)).astype(BF16)
    send(e2, zb, dev(z=zo), r_zb)
    sum_pass(afull, 0, H, bufs_a, r_xa)
    sum_pass(afull, H, BLOCK - H, bufs_c, r_xc)

    def cols_of(x, z, n=256):
        return at(c * 2048 + z * 1024 + x * 256, n)

    total = afull[:H, mycols] + sum_end(H, bufs_a, r_xa)
    out[:H, cols_of(x, z)] = (total * SCALE).astype(BF16)

    arrived(zb, r_zb)
    total = afull[H:, mycols] + zb[...].astype(F32) + sum_end(BLOCK - H, bufs_c, r_xc)
    out[H:, cols_of(x, z)] = (total * SCALE).astype(BF16)
    top, low = (0, TOP), (TOP, BLOCK - TOP)
    kinds = ((top, z), (low, z), (low, zo))
    cores = []

    def piece(rows, gx, gz, half=None, gc=c):
        start, size = rows
        if half is not None:
            start, size = start + half * (size // 2), size // 2
        return out.at[pl.ds(start, size), at(gc * 2048 + gz * 1024 + gx * 256, 256)]

    def across(rows, gx, gz, half=None):
        ref = piece(rows, gx, gz, half)
        send(ref, ref, dev(c=co), r_oc.at[len(cores)])
        cores.append((rows, gx, gz, half))

    def round_x(i):
        ref = piece(kinds[i][0], x, kinds[i][1])
        send(ref, ref, dev(x=right), r_ox.at[i * 4])
        send(ref, ref, dev(x=left), r_ox.at[i * 4 + 1])

    def pass_on(i):
        rows, gz = kinds[i]
        for g, half, to, n in ((left, 0, right, 0), (right, 1, left, 1)):
            arrived(piece(rows, g, gz), r_ox.at[i * 4 + n])
            ref = piece(rows, g, gz, half)
            send(ref, ref, dev(x=to), r_ox.at[i * 4 + 2 + n])
            if i == 0:
                over_z(g)
            across(rows, g, gz)

    def last(i):
        rows, gz = kinds[i]
        for half in range(2):
            arrived(piece(rows, far, gz, half), r_ox.at[i * 4 + 2 + half])
            if i == 0:
                over_z(far, half)
            across(rows, far, gz, half)

    overs = []

    def over_z(g, half=None):
        ref = piece(top, g, z, half)
        send(ref, ref, dev(z=zo), r_oz.at[len(overs)])
        overs.append((g, half))

    mine = piece(low, x, z)
    send(mine, mine, dev(z=zo), r_oz.at[5])
    round_x(0)
    over_z(x)
    round_x(1)
    across(top, x, z)
    across(low, x, z)
    pass_on(0)
    arrived(piece(low, x, zo), r_oz.at[5])
    round_x(2)
    across(low, x, zo)
    pass_on(1)
    pass_on(2)
    last(0)
    last(1)
    last(2)
    for n, (g, half) in enumerate(overs):
        arrived(piece(top, g, zo, half), r_oz.at[n])
        across(top, g, zo, half)
    for n, (rows, gx, gz, half) in enumerate(cores):
        arrived(piece(rows, gx, gz, half, co), r_oc.at[n])
    for sent in pending:
        if sent is not None:
            when(sent[1], sent[0].wait_send)


def shards(tokens, basis):
    dma = pltpu.SemaphoreType.DMA
    vm = pltpu.VMEM
    out, proj = pl.pallas_call(
        kernel,
        out_shape=(
            pltpu.VMEM((BLOCK, WIDTH), BF16),
            pltpu.VMEM((ROWS, BLOCK), F32),
        ),
        in_specs=[pl.BlockSpec(memory_space=pl.ANY)] * 2,
        out_specs=(pl.BlockSpec(memory_space=pltpu.VMEM), pl.BlockSpec(memory_space=pltpu.VMEM)),
        scratch_shapes=[
            vm((ROWS, WIDTH), BF16),
            vm((ROWS, 2048), BF16),
            vm((BLOCK, WIDTH), BF16),
            vm((512, 1024), BF16),
            vm((ROWS, BLOCK), BF16),
            vm((4, ROWS, 128), BF16),
            vm((4, ROWS, 128), BF16),
            vm((3, 2, 2, 32, 512), BF16),
            vm((3, 2, 32, 512), BF16),
            vm((3, 2, 32, 512), BF16),
            vm((8, 3, 32, 128), BF16),
            vm((6, 8, 2, 32, 128), BF16),
            vm((2, 4, ROWS, BLOCK), BF16),
            vm((4, 128, BLOCK), BF16),
            vm((8, 4, 32, 128), BF16),
            vm((4, BLOCK, 128), BF16),
            vm((2, BLOCK, ROWS), BF16),
            vm((BLOCK, 1024), BF16),
            vm((BLOCK, 1024), F32),
            vm((H, 1024), BF16),
            vm((H, 1024), BF16),
            vm((BLOCK - H, 1024), BF16),
            vm((2, H // 2, 256), BF16),
            vm((2, H // 2, 256), BF16),
            vm((2, H, 256), BF16),
            vm((2, (BLOCK - H) // 2, 256), BF16),
            vm((2, (BLOCK - H) // 2, 256), BF16),
            vm((2, BLOCK - H, 256), BF16),
            vm((2, (BLOCK - H) // 2, 256), BF16),
            vm((2, (BLOCK - H) // 2, 256), BF16),
            vm((2, BLOCK - H, 256), BF16),
            vm((BLOCK - H, 256), BF16),
            vm((BLOCK - H, 256), BF16),
            dma((300,)),
            dma((3,)),
            dma,
            dma((4,)),
            dma((4,)),
            dma((4,)),
            dma((16,)),
            dma((4,)),
            dma((32,)),
            dma((4,)),
            dma((16 * PARTS,)),
            dma((4 * PARTS,)),
            dma((8,)),
            dma((16,)),
            dma,
            dma((6,)),
            dma((6,)),
            dma((6,)),
            dma,
            dma((12,)),
            dma((6,)),
            dma((24,)),
            dma((4,)),
            dma,
            dma((8,)),
        ],
        compiler_params=pltpu.CompilerParams(
            collective_id=0, has_side_effects=True, vmem_limit_bytes=56 << 20
        ),
        name="sanger",
    )(tokens, basis)
    return out, proj


def solution(mesh):
    in_specs = (P("dp", "feat"), P("section", "feat"))
    out_specs = (P("section", "feat"), P("dp", "section"))
    return jax.shard_map(shards, mesh=mesh, in_specs=in_specs, out_specs=out_specs, check_vma=False)
```
